32 devices in a mesh: users: 8 (over z, x), items: 4 (over y, core).
Axes of the slice: x: 2, y: 2, z: 4, core: 2. Of those that a mesh axis runs over, the one named last changes fastest.
Arguments:
- tile_users: int32 [8, 4, 128], P('users', 'items'), may hold values from 0 to 127
- tile_owners: int32 [8, 4, 128, 1], P('users', 'items'), may hold values from 0 to 7; in each aligned block of 128 rows (0 to 127, 128 to 255, ..., all dimensions but the last counted through in order) at most 32 rows name the same one
- tile_blocks: int32 [8, 4, 128], P('users', 'items'), may hold values from 0 to 63
- tile_contexts: int32 [8, 4, 128], P('users', 'items'), may hold values from 0 to 7
- row_users: int32 [8, 4, 128, 128], P('users', 'items'), may hold values from 0 to 15
- row_items: int32 [8, 4, 128, 128], P('users', 'items'), may hold values from 0 to 15
- row_contexts: int32 [8, 4, 128, 128], P('users', 'items'), may hold values from 0 to 127
- tile_values: bfloat16 [8, 4, 128, 128], P('users', 'items'), may hold values from -49152 to 49152
- tile_count: int32 [8, 4], P('users', 'items'), may hold values from 64 to 128, as said below
- item_factors: bfloat16 [8192, 256], P('users'), may hold values from -0.125 to 0.25
- context_factors: bfloat16 [1024, 256], replicated, may hold values from -0.125 to 0.25
- profile: bfloat16 [16384, 2048], P('users', 'items'), may hold values from -192 to 192
- feature_factors: bfloat16 [2048, 256], P('items'), may hold values from -6 to 6
Outputs:
- user_factors: bfloat16 [16384, 256], P('users')
- feature_new: bfloat16 [2048, 256], P('items')
The draws below stay inside these ranges and needn't reach their ends.
Inputs may be any that keep to these rules, and one draw needn't show every extreme that they name: On one device at most 32 tiles name one index of users in tile_owners, a bound that some block reaches. The live tiles of a device are its first tile_count tiles; some device has all 128 live.
All inputs are finite; a program needn't handle non-finite values.
Results may differ from the reference program's by a relative error of at most 0.00155.
The reference program's roundings to bfloat16 on the way count: a program that leaves them out, or rounds other values in their place, can miss the bound.
Values may be sent and summed in bfloat16 or wider, within the bound.
No kernel may reach another device: no remote copies, remote signals or barrier semaphores. Data moves between devices by JAX's collectives and lax.ppermute only.
A program may use at most 64 MiB of HBM per device.

```python
import math
import jax
import jax.numpy as jnp
import numpy as np
from jax import lax

R = 256
FEAT = 2048
CTX = 1024
CB = 128
IB = 16
UB = 16
TR = 128
U_DEV = 2048
TILES_DEV = 128
CAP = 32
BLK_OWN = 64
USERS = 16384
NI = 8192
N_USERS = 8
N_ITEMS = 4


def draw_tile_count(key, part):
    first_key, second_key = jax.random.split(jax.random.fold_in(key, 17))
    divisor_table = jnp.array([1, 1, 1, 2], dtype=jnp.int32)
    picks = jax.random.randint(first_key, (N_USERS * N_ITEMS,), 0, 4)
    counts = TILES_DEV // divisor_table[picks]
    full_at = jax.random.randint(second_key, (), 0, N_USERS * N_ITEMS)
    counts = jnp.where(jnp.arange(N_USERS * N_ITEMS) == full_at, TILES_DEV, counts)
    return counts.reshape(N_USERS, N_ITEMS).astype(jnp.int32)


def with_ends(values, stream_key, smallest, high):
    longest = values.shape.index(max(values.shape))
    spots = []
    for shift in (0, 1):
        where = [jax.random.randint(jax.random.fold_in(stream_key, axis), (), 0, length) for axis, length in enumerate(values.shape)]
        where[longest] = (where[longest] + shift) % values.shape[longest]
        spots.append(tuple(where))
    return values.at[spots[0]].set(smallest).at[spots[1]].set(high)


def steps_of(own_key, extent, cuts, least, high):
    factor_of = 1.0
    for axis_at, shards_of in cuts:
        draws = jax.random.uniform(jax.random.fold_in(jax.random.fold_in(own_key, 6), axis_at), (shards_of,), jnp.float32, least / len(cuts), high / len(cuts))
        factor_of = factor_of * jnp.repeat(jnp.exp(draws), extent[axis_at] // shards_of).reshape((-1,) + (1,) * (len(extent) - 1 - axis_at))
    return factor_of


def shared_out(stream_key, own, number, rows, number_of, top, most, skew):
    order = jax.random.permutation(stream_key, number_of)
    crowded, ordinary = portions_of(number_of, rows * top, most, skew, True), portions_of(number_of, rows * top, most, skew, False)
    places = jnp.arange(number_of)

    def named(sizes, offset_by):
        used = int((sizes > 0).sum())
        fixed = max(1, used // 4)
        passed = fixed + (places - fixed + offset_by * (used - fixed)) % max(1, number_of - fixed)
        return jnp.zeros((number_of,), jnp.int32).at[order[jnp.where(places < fixed, places, passed)]].set(jnp.asarray(sizes, jnp.int32))

    sizes = jnp.where(number % 4 == 0, named(crowded, number // 4), named(ordinary, number - number // 4 - 1))
    mixed = jax.random.permutation(jax.random.fold_in(own, 3), number_of)
    source_of, sink = mixed[0:number_of // 2 * 2:2], mixed[1:number_of // 2 * 2:2]
    slack = jnp.minimum(sizes[source_of] - 1, most - sizes[sink]) // 2
    slack = jnp.where((source_of == order[0]) | (sink == order[0]) | (sizes[sink] == 0), 0, jnp.maximum(slack, 0))
    passed = jax.random.randint(jax.random.fold_in(own, 4), (number_of // 2,), 0, 1 << 20) % (slack + 1)
    sizes = sizes.at[source_of].add(-passed).at[sink].add(passed)
    members = jnp.searchsorted(jnp.cumsum(sizes), jnp.arange(rows * top), side="right").astype(jnp.int32)
    grid = members.reshape(top, rows).T
    grid = grid[jax.random.permutation(jax.random.fold_in(own, 1), rows)]
    offset_by = jax.random.randint(jax.random.fold_in(own, 2), (rows, 1), 0, top)
    return jnp.take_along_axis(grid, (jnp.arange(top)[None, :] + offset_by) % top, axis=1)


def portions_of(amount, total, limit, slope, full):
    weights = [(1 << 20) // math.isqrt(grade ** slope) + 1 for grade in range(1, amount + 1)]
    largest = limit if full else min(limit, max(-(-total // amount), total * weights[0] // sum(weights)))
    least = 1 if total - largest >= amount - 1 else 0
    given, spare = [largest] + [least] * (amount - 1), total - largest - least * (amount - 1)
    while spare > 0:
        movable = [i for i in range(1, amount) if given[i] < largest] or [i for i in range(1, amount) if given[i] < limit]
        whole, remaining = sum([weights[i] for i in movable]), spare
        for i in movable:
            more = min(limit - given[i], max(1, remaining * weights[i] // whole), spare)
            given[i] = given[i] + more
            spare = spare - more
    return np.array(given)


def centred(rng, shape, scale, bound, shards=(), kind=jnp.bfloat16):
    result = scale * jax.random.normal(rng, shape, jnp.float32)
    if shards:
        result = result * steps_of(rng, shape, shards, -0.22, 0.18)
    return jnp.clip(result, -bound, bound).astype(kind)


def setup_inputs(seed: int = 0) -> dict:
    key_of = jax.random.split(jax.random.key(seed), 14)
    tile_users = with_ends(jax.random.randint(key_of[0], (N_USERS, N_ITEMS, TILES_DEV), 0, U_DEV // UB), jax.random.fold_in(key_of[0], 1), 0, (U_DEV // UB) - 1).astype(jnp.int32)
    tile_owners_keys = jax.random.split(jax.random.fold_in(key_of[1], 1), N_USERS * N_ITEMS * TILES_DEV // TILES_DEV)
    tile_owners_turns = jax.random.permutation(jax.random.fold_in(key_of[1], 3), N_USERS * N_ITEMS * TILES_DEV // TILES_DEV)
    tile_owners = jax.vmap(lambda own, number: shared_out(jax.random.fold_in(key_of[1], 2), own, number, TILES_DEV, N_USERS, 1, CAP, 2))(tile_owners_keys, tile_owners_turns).reshape((N_USERS, N_ITEMS, TILES_DEV, 1))
    tile_blocks = with_ends(jax.random.randint(key_of[2], (N_USERS, N_ITEMS, TILES_DEV), 0, BLK_OWN), jax.random.fold_in(key_of[2], 1), 0, BLK_OWN - 1).astype(jnp.int32)
    tile_contexts = with_ends(jax.random.randint(key_of[3], (N_USERS, N_ITEMS, TILES_DEV), 0, CTX // CB), jax.random.fold_in(key_of[3], 1), 0, (CTX // CB) - 1).astype(jnp.int32)
    row_users = with_ends(jax.random.randint(key_of[4], (N_USERS, N_ITEMS, TILES_DEV, TR), 0, UB), jax.random.fold_in(key_of[4], 1), 0, UB - 1).astype(jnp.int32)
    row_items = with_ends(jax.random.randint(key_of[5], (N_USERS, N_ITEMS, TILES_DEV, TR), 0, IB), jax.random.fold_in(key_of[5], 1), 0, IB - 1).astype(jnp.int32)
    row_contexts = with_ends(jax.random.randint(key_of[6], (N_USERS, N_ITEMS, TILES_DEV, TR), 0, CB), jax.random.fold_in(key_of[6], 1), 0, CB - 1).astype(jnp.int32)
    tile_values = centred(key_of[7], (N_USERS, N_ITEMS, TILES_DEV, TR), 8192.0, 49152.0, ((0, 8), (1, 4)))
    tile_count = draw_tile_count(jax.random.fold_in(key_of[13], 71), 0)
    item_factors = jnp.clip(-0.125 + 0.375 * jax.random.uniform(key_of[9], (NI, R), jnp.float32) ** steps_of(key_of[9], (NI, R), ((0, 8),), -0.2, 0.2), -0.125, 0.25).astype(jnp.bfloat16)
    context_factors = jnp.clip(jax.random.uniform(key_of[10], (CTX, R), jnp.float32, -0.125, 0.25), -0.125, 0.25).astype(jnp.bfloat16)
    profile = centred(key_of[11], (USERS, FEAT), 32.0, 192.0, ((0, 8), (1, 4)))
    feature_factors = centred(key_of[12], (FEAT, R), 1.0, 6.0, ((0, 4),))
    return {"tile_users": tile_users, "tile_owners": tile_owners, "tile_blocks": tile_blocks, "tile_contexts": tile_contexts, "row_users": row_users, "row_items": row_items, "row_contexts": row_contexts, "tile_values": tile_values, "tile_count": tile_count, "item_factors": item_factors, "context_factors": context_factors, "profile": profile, "feature_factors": feature_factors}


RIDGE = 1.0

def gram(matrix):
    return lax.dot_general(matrix.astype(jnp.float32), matrix.astype(jnp.float32), (((0,), (0,)), ((), ())), preferred_element_type=jnp.float32)

def solve_rows(normal, right_side):
    cholesky_factor = jnp.linalg.cholesky(normal)
    return jax.scipy.linalg.cho_solve((cholesky_factor, True), right_side.T).T

def reference(tile_users, tile_owners, tile_blocks, tile_contexts, row_users, row_items, row_contexts, tile_values, tile_count, item_factors, context_factors, profile, feature_factors):
    devices_all = N_USERS * N_ITEMS

    def per_device(pieces):
        t_users, t_owners, t_blocks, t_ctx, r_users, r_items, r_ctx, values, live_count = pieces
        alive = (jnp.arange(TILES_DEV, dtype=jnp.int32) < live_count).astype(jnp.float32)
        users_local = t_users[:, None] * UB + r_users
        items_global = (t_owners[:, 0] * BLK_OWN + t_blocks)[:, None] * IB + r_items
        ctx_global = t_ctx[:, None] * CB + r_ctx
        weighted = values.astype(jnp.float32) * alive[:, None]
        row_terms = weighted[:, :, None] * item_factors[items_global].astype(jnp.float32) * context_factors[ctx_global].astype(jnp.float32)
        return jax.ops.segment_sum(row_terms.reshape(-1, R), users_local.reshape(-1).astype(jnp.int32), num_segments=U_DEV)
    pieces = (tile_users.reshape(devices_all, TILES_DEV), tile_owners.reshape(devices_all, TILES_DEV, 1), tile_blocks.reshape(devices_all, TILES_DEV), tile_contexts.reshape(devices_all, TILES_DEV), row_users.reshape(devices_all, TILES_DEV, TR), row_items.reshape(devices_all, TILES_DEV, TR), row_contexts.reshape(devices_all, TILES_DEV, TR), tile_values.reshape(devices_all, TILES_DEV, TR), tile_count.reshape(devices_all))
    partial_terms = lax.map(per_device, pieces)
    mttkrp = jnp.sum(partial_terms.reshape(N_USERS, N_ITEMS, U_DEV, R), axis=1).reshape(USERS, R)
    right_side = mttkrp + jnp.dot(profile.astype(jnp.float32), feature_factors.astype(jnp.float32), preferred_element_type=jnp.float32)
    identity = jnp.eye(R, dtype=jnp.float32)
    normal = gram(item_factors) * gram(context_factors) + gram(feature_factors) + RIDGE * identity
    user_factors = solve_rows(normal, right_side).astype(jnp.bfloat16)
    user_gram = gram(user_factors) + RIDGE * identity
    feature_right = lax.dot_general(profile.astype(jnp.float32), user_factors.astype(jnp.float32), (((0,), (0,)), ((), ())), preferred_element_type=jnp.float32)
    feature_new = solve_rows(user_gram, feature_right).astype(jnp.bfloat16)
    return (user_factors, feature_new)
```

```python
import jax
import jax.numpy as jnp
from jax import lax
from jax.experimental import pallas as pl
from jax.experimental.pallas import tpu as pltpu
from jax.sharding import PartitionSpec as P

CB = 128
IB = 16
UB = 16
SLAB = 128
RIDGE = 1.0
UNROLL = 8
HI = lax.Precision.HIGHEST
VM = pl.BlockSpec(memory_space=pltpu.VMEM)
SM = pl.BlockSpec(memory_space=pltpu.SMEM)


def gram(matrix):
    return lax.dot_general(
        matrix, matrix, (((0,), (0,)), ((), ())), preferred_element_type=jnp.float32
    )

def mm(a, b, dims=(((1,), (0,)), ((), ()))):
    return lax.dot_general(a, b, dims, precision=HI, preferred_element_type=jnp.float32)

def base_inverse(a):
    n = a.shape[0]
    rows = lax.broadcasted_iota(jnp.int32, (n, n), 0)
    lanes = lax.broadcasted_iota(jnp.int32, (n, n), 1)
    lane1 = lax.broadcasted_iota(jnp.int32, (1, n), 1)
    for k in range(n):
        col = jnp.broadcast_to(a[:, k:k+1], (n, n))
        p = 1.0 / col[k:k+1, :]
        row = jnp.where(lane1 == k, p, a[k:k+1, :] * p)
        upd = jnp.where(lanes == k, 0.0, a) - col * row
        a = jnp.where(rows == k, jnp.broadcast_to(row, (n, n)), upd)
    return a

def inverse_value(a):
    n = a.shape[0]
    if n <= 128:
        return base_inverse(a)
    h = n // 2
    a11, a12, a22 = a[:h, :h], a[:h, h:], a[h:, h:]
    i11 = inverse_value(a11)
    w = mm(i11, a12)
    s = a22 - mm(a12, w, (((0,), (0,)), ((), ())))
    i22 = inverse_value(s)
    b12 = -mm(w, i22)
    b11 = i11 - mm(b12, w, (((1,), (1,)), ((), ())))
    b21 = -mm(i22, w, (((1,), (1,)), ((), ())))
    return jnp.concatenate([jnp.concatenate([b11, b12], 1), jnp.concatenate([b21, i22], 1)], 0)

def inverse_kernel(a_ref, o_ref):
    o_ref[...] = inverse_value(a_ref[...])

def inverse(a):
    return pl.pallas_call(inverse_kernel, out_shape=jax.ShapeDtypeStruct(a.shape, jnp.float32), in_specs=[VM], out_specs=VM)(a)

def tiles_kernel(meta_own, meta_par, own_ref, par_ref, table_ref, ctx_ref, out_ref, data_ref):
    bf = jnp.bfloat16
    ib = out_ref.shape[1]
    out_ref[...] = jnp.zeros_like(out_ref)
    width = own_ref.shape[2]
    big = lax.broadcasted_iota(jnp.int32, (width, width), 0).astype(jnp.float32).astype(bf)
    small = lax.broadcasted_iota(jnp.int32, (16, width), 0).astype(jnp.float32).astype(bf)
    one, zero = jnp.ones((), bf), jnp.zeros((), bf)
    for meta, src in ((meta_own, own_ref), (meta_par, par_ref)):
        data_ref[...] = src[...].astype(jnp.float32)
        def group(g, _):
            first = pl.multiple_of(g * UNROLL, UNROLL)
            us, its, cs, vs = (data_ref[j, pl.ds(first, UNROLL), :] for j in range(4))
            for j in range(UNROLL):
                t = first + j
                def row(x, h):
                    return jnp.broadcast_to(x[j:j+1, :].astype(bf), (h, width))
                oh_i = jnp.where(row(its, width) == big, one, zero)
                oh_c = jnp.where(row(cs, width) == big, one, zero)
                s = jnp.where(row(us, 16) == small, row(vs, 16), zero)
                a = jnp.dot(table_ref[meta[0, t]], oh_i, preferred_element_type=jnp.float32)
                b = jnp.dot(ctx_ref[meta[1, t]], oh_c, preferred_element_type=jnp.float32)
                p = a * b
                hi = p.astype(bf)
                lo = (p - hi.astype(jnp.float32)).astype(bf)
                nt = (((1,), (1,)), ((), ()))
                r = lax.dot_general(s, hi, nt, preferred_element_type=jnp.float32) + lax.dot_general(s, lo, nt, preferred_element_type=jnp.float32)
                at = pl.ds(pl.multiple_of(meta[2, t], 16), 16)
                out_ref[at, :] += r
            return 0
        lax.fori_loop(0, (meta[3, 0] + UNROLL - 1) // UNROLL, group, 0)

def tiles(meta_own, meta_par, own, par, table, ctx, users):
    return pl.pallas_call(tiles_kernel,
        out_shape=jax.ShapeDtypeStruct((users, table.shape[1]), jnp.float32),
        in_specs=[SM, SM, VM, VM, VM, VM], out_specs=VM,
        scratch_shapes=[pltpu.VMEM(own.shape, jnp.float32)])(meta_own, meta_par, own, par, table, ctx)


def swap(x, axis, distance):
    size = lax.axis_size(axis)
    return lax.ppermute(x, axis, [(i, i ^ distance) for i in range(size)])


def halves(size):
    steps = []
    while size > 1:
        size //= 2
        steps.append(size)
    return steps


def take_rows(x, start, count):
    return lax.dynamic_slice_in_dim(x, start, count, 0)


def item_order():
    items_size = lax.axis_size("items")
    me = lax.axis_index("items")
    top = items_size // 2
    low, high = me % top, me // top
    return items_size, top, low, high


def scatter_items(x):
    items_size, top, low, high = item_order()
    me = lax.axis_index("items")
    for distance in halves(top) + [top]:
        half = x.shape[0] // 2
        bit = (me // distance) % 2
        keep = take_rows(x, bit * half, half)
        send = take_rows(x, (1 - bit) * half, half)
        x = keep + swap(send, "items", distance)
    return x


def gather_items(x):
    items_size, top, low, high = item_order()
    me = lax.axis_index("items")
    for distance in [top] + halves(top)[::-1]:
        bit = (me // distance) % 2
        other = swap(x, "items", distance)
        x = jnp.concatenate(
            [jnp.where(bit == 0, x, other), jnp.where(bit == 0, other, x)], 0
        )
    return x


def sum_users(x):
    for distance in halves(lax.axis_size("users"))[::-1]:
        x = x + swap(x, "users", distance)
    return x


def scatter_users(x):
    size = lax.axis_size("users")
    me = lax.axis_index("users")
    rows = x.shape[0] // size
    if size > 16:
        return lax.psum_scatter(x, "users", scatter_dimension=0, tiled=True)
    total = take_rows(x, me * rows, rows)
    for distance in range(1, size):
        total = total + swap(take_rows(x, (me ^ distance) * rows, rows), "users", distance)
    return total


def gather_users(x):
    size = lax.axis_size("users")
    me = lax.axis_index("users")
    if size > 16:
        return lax.all_gather(x, "users", tiled=True)
    rows = x.shape[0]
    out = jnp.zeros((size * rows,) + x.shape[1:], x.dtype)
    for distance in range(size):
        piece = x if distance == 0 else swap(x, "users", distance)
        out = lax.dynamic_update_slice_in_dim(out, piece, (me ^ distance) * rows, 0)
    return out


def gather_table(item_factors):
    items_size, top, low, high = item_order()
    size = lax.axis_size("users")
    me = lax.axis_index("users")
    rows, width = item_factors.shape
    cols = width // 2
    mine = lax.dynamic_slice_in_dim(item_factors, high * cols, cols, 1)
    if size > 16 or rows % (SLAB * top):
        full = lax.all_gather(mine, "users", tiled=True)
        table = full.reshape(-1, SLAB, cols).transpose(0, 2, 1)
        return table, lambda slab: slab
    slabs = mine.reshape(rows // SLAB, SLAB, cols).transpose(0, 2, 1)
    part = rows // SLAB // top
    piece = take_rows(slabs, low * part, part)
    parts = [piece] + [swap(piece, "users", d) for d in range(1, size)]
    table = jnp.concatenate(parts, 0)
    for distance in halves(top)[::-1]:
        table = jnp.concatenate([table, swap(table, "items", distance)], 0)
    held = rows // SLAB

    def place(slab):
        owner, inner = slab // held, slab % held
        return ((inner // part) ^ low) * (size * part) + (owner ^ me) * part + inner % part

    return table, place


def local(
    tile_users,
    tile_owners,
    tile_blocks,
    tile_contexts,
    row_users,
    row_items,
    row_contexts,
    tile_values,
    tile_count,
    item_factors,
    context_factors,
    profile,
    feature_factors,
):
    items_size, top, low, high = item_order()
    tile_total = tile_users.shape[2]
    rank_width = item_factors.shape[1]
    cols = rank_width // 2
    slab_users = profile.shape[0]
    blocks_held = item_factors.shape[0] // IB
    bf16 = jnp.bfloat16

    table, place = gather_table(item_factors)
    contexts = lax.dynamic_slice_in_dim(context_factors, high * cols, cols, 1)
    contexts = contexts.reshape(-1, CB, cols).transpose(0, 2, 1)

    live = tile_count.reshape(())
    block = (tile_owners.reshape(tile_total) * blocks_held + tile_blocks.reshape(tile_total))
    per_slab = SLAB // IB
    meta = jnp.stack(
        [
            place(block // per_slab),
            tile_contexts.reshape(tile_total),
            tile_users.reshape(tile_total) * UB,
            jnp.broadcast_to(live, (tile_total,)),
        ]
    )
    alive = (jnp.arange(tile_total, dtype=jnp.int32) < live)[:, None]
    width = row_users.shape[3]
    shape = (tile_total, width)
    data = jnp.stack(
        [
            row_users.reshape(shape).astype(bf16),
            (row_items.reshape(shape) + (block % per_slab * IB)[:, None]).astype(bf16),
            row_contexts.reshape(shape).astype(bf16),
            jnp.where(alive, tile_values.reshape(shape), jnp.zeros((), bf16)),
        ]
    )
    meta_other = swap(meta, "items", top)
    data_other = swap(data, "items", top)

    item_part = scatter_rows(gram(item_factors))
    feature_part = scatter_items(gram(feature_factors))
    context_part = scatter_rows(gram(context_factors))
    item_part = sum_users(item_part)
    own_rows = item_part.shape[0]
    first_row = quarter() * own_rows
    diagonal = (
        first_row + lax.broadcasted_iota(jnp.int32, item_part.shape, 0)
        == lax.broadcasted_iota(jnp.int32, item_part.shape, 1)
    ).astype(jnp.float32)
    normal = gather_items(item_part * context_part + feature_part + RIDGE * diagonal)
    normal_inverse = inverse(normal)

    dense = scatter_items(
        jnp.dot(profile, feature_factors, preferred_element_type=jnp.float32)
    )
    sparse = tiles(meta, meta_other, data, data_other, table, contexts, slab_users)
    for distance in halves(top):
        half = sparse.shape[0] // 2
        bit = (lax.axis_index("items") // distance) % 2
        keep = take_rows(sparse, bit * half, half)
        sparse = keep + swap(take_rows(sparse, (1 - bit) * half, half), "items", distance)
    half = sparse.shape[0] // 2
    mine = take_rows(sparse, high * half, half)
    other = swap(take_rows(sparse, (1 - high) * half, half), "items", top)
    sparse = jnp.concatenate(
        [jnp.where(high == 0, mine, other), jnp.where(high == 0, other, mine)], 1
    )
    right_part = sparse + dense
    users_part = jnp.dot(right_part, normal_inverse, precision=lax.Precision.HIGHEST)
    users_part = users_part.astype(bf16)

    user_gram = gather_items(sum_users(scatter_items(gram(users_part))))
    identity = jnp.eye(rank_width, dtype=jnp.float32)
    user_inverse = inverse(user_gram + RIDGE * identity)
    user_factors = gather_items(users_part)
    feature_terms = lax.dot_general(
        profile, user_factors, (((0,), (0,)), ((), ())), preferred_element_type=jnp.float32
    )
    feature_right = scatter_users(feature_terms)
    feature_part = jnp.dot(feature_right, user_inverse, precision=lax.Precision.HIGHEST)
    feature_new = gather_users(feature_part.astype(bf16))
    return (user_factors, feature_new)


def quarter():
    items_size, top, low, high = item_order()
    me = lax.axis_index("items")
    index = 0
    for distance in halves(top) + [top]:
        index = index * 2 + (me // distance) % 2
    return index


def scatter_rows(x):
    rows = x.shape[0] // lax.axis_size("items")
    return take_rows(x, quarter() * rows, rows)


def solution(mesh):
    in_specs = (
        P("users", "items", None),
        P("users", "items", None, None),
        P("users", "items", None),
        P("users", "items", None),
        P("users", "items", None, None),
        P("users", "items", None, None),
        P("users", "items", None, None),
        P("users", "items", None, None),
        P("users", "items"),
        P("users", None),
        P(),
        P("users", "items"),
        P("items", None),
    )
    out_specs = (P("users", None), P("items", None))
    return jax.shard_map(local, mesh=mesh, in_specs=in_specs, out_specs=out_specs, check_vma=False)
```

```python
import jax
import jax.numpy as jnp
from jax import lax
from jax.experimental import pallas as pl
from jax.experimental.pallas import tpu as pltpu
from jax.sharding import PartitionSpec as P

CB = 128
IB = 16
UB = 16
SLAB = 128
RIDGE = 1.0
UNROLL = 32
PIVOTS = 8
HI = lax.Precision.HIGHEST
VM = pl.BlockSpec(memory_space=pltpu.VMEM)
SM = pl.BlockSpec(memory_space=pltpu.SMEM)
ANY = pl.BlockSpec(memory_space=pl.ANY)
F32 = jnp.float32
BF16 = jnp.bfloat16


def gram(matrix):
    return lax.dot_general(
        matrix, matrix, (((0,), (0,)), ((), ())), preferred_element_type=F32
    )


def mm(a, b, dims=(((1,), (0,)), ((), ()))):
    return lax.dot_general(a, b, dims, precision=HI, preferred_element_type=F32)


def solve_pivots(d, r):
    n = len(r)
    if n == 1:
        return [r[0] * (1.0 / d[0][0])]
    h = n // 2
    if n == 2:
        p = 1.0 / d[0][0]
        low = d[0][1] * p
        q = 1.0 / (d[1][1] - d[0][1] * low)
        last = (r[1] - low * r[0]) * q
        return [r[0] * p - low * last, last]
    first = [[d[i][j] if j >= i else None for j in range(h)] for i in range(h)]
    cross = [[d[i][h + j] for j in range(h)] for i in range(h)]
    t = solve_pivots(first, r[:h])
    w = [solve_pivots(first, [cross[i][j] for i in range(h)]) for j in range(h)]
    schur = [
        [
            d[h + i][h + j] - sum(cross[m][i] * w[j][m] for m in range(h)) if j >= i else None
            for j in range(h)
        ]
        for i in range(h)
    ]
    rest = [r[h + i] - sum(cross[m][i] * t[m] for m in range(h)) for i in range(h)]
    q = solve_pivots(schur, rest)
    return [t[m] - sum(w[j][m] * q[j] for j in range(h)) for m in range(h)] + q


def base_inverse(a):
    n = a.shape[0]
    lanes = lax.broadcasted_iota(jnp.int32, (PIVOTS, n), 1)
    lane1 = lax.broadcasted_iota(jnp.int32, (1, n), 1)
    blocks = [a[PIVOTS * i : PIVOTS * (i + 1), :] for i in range(n // PIVOTS)]

    def columns(block, k):
        return [jnp.broadcast_to(block[:, k + j : k + j + 1], (PIVOTS, n)) for j in range(PIVOTS)]

    for v in range(n // PIVOTS):
        k = v * PIVOTS
        pivot = columns(blocks[v], k)
        d = [[pivot[j][i : i + 1, :] for j in range(PIVOTS)] for i in range(PIVOTS)]
        inside = (lane1 >= k) & (lane1 < k + PIVOTS)
        r = [
            jnp.where(inside, (lane1 == k + i).astype(F32), blocks[v][i : i + 1, :])
            for i in range(PIVOTS)
        ]
        rows = [jnp.broadcast_to(x, (PIVOTS, n)) for x in solve_pivots(d, r)]
        inside = (lanes >= k) & (lanes < k + PIVOTS)
        new = []
        for i, block in enumerate(blocks):
            if i == v:
                sub = lax.broadcasted_iota(jnp.int32, (PIVOTS, n), 0)
                x = rows[0]
                for j in range(1, PIVOTS):
                    x = jnp.where(sub == j, rows[j], x)
            else:
                c = columns(block, k)
                x = jnp.where(inside, 0.0, block)
                u = c[0] * rows[0]
                for j in range(1, PIVOTS):
                    u = u + c[j] * rows[j]
                x = x - u
            new.append(x)
        blocks = new
    return jnp.concatenate(blocks, 0)


def inverse_value(a):
    n = a.shape[0]
    if n <= 128:
        return base_inverse(a)
    h = n // 2
    a12 = a[:h, h:]
    i11 = inverse_value(a[:h, :h])
    w = mm(i11, a12)
    i22 = inverse_value(a[h:, h:] - mm(a12, w, (((0,), (0,)), ((), ()))))
    nt = (((1,), (1,)), ((), ()))
    b12 = -mm(w, i22)
    b11 = i11 - mm(b12, w, nt)
    b21 = -mm(i22, w, nt)
    return jnp.concatenate(
        [jnp.concatenate([b11, b12], 1), jnp.concatenate([b21, i22], 1)], 0
    )


def inverse_kernel(a_ref, o_ref):
    o_ref[...] = inverse_value(a_ref[...])


def inverse(a):
    return pl.pallas_call(
        inverse_kernel,
        out_shape=jax.ShapeDtypeStruct(a.shape, F32),
        in_specs=[VM],
        out_specs=VM,
    )(a)


def prep_kernel(place, blocks_held, ids, count, owners, blocks, contexts, users, ru, ri, rc, val, meta, data):
    tiles_here, width = ru.shape
    shape = (tiles_here, tiles_here)
    eye = lax.broadcasted_iota(jnp.int32, shape, 0) == lax.broadcasted_iota(jnp.int32, shape, 1)
    owner = jnp.sum(jnp.where(eye, owners[...], 0), axis=0, keepdims=True)
    per_slab = SLAB // IB
    block = owner * blocks_held + blocks[...]
    rows = [
        place(block // per_slab, ids),
        contexts[...],
        users[...] * UB,
        block % per_slab * IB,
        jnp.full((1, tiles_here), count[0, 0], jnp.int32),
    ]
    for i, row in enumerate(rows):
        meta[i : i + 1, :] = row
    meta[len(rows) :, :] = jnp.zeros((8 - len(rows), tiles_here), jnp.int32)
    alive = lax.broadcasted_iota(jnp.int32, (tiles_here, width), 0) < count[0, 0]
    data[0] = ru[...].astype(F32).astype(BF16)
    data[1] = ri[...].astype(F32).astype(BF16)
    data[2] = rc[...].astype(F32).astype(BF16)
    data[3] = jnp.where(alive, val[...].astype(F32), 0.0).astype(BF16)


def tiles_kernel(n_tables, ids, meta_own, meta_par, own_ref, par_ref, ctx_ref, *rest):
    tables = rest[:n_tables]
    outs = rest[n_tables : n_tables + 3]
    table_ref, data_ref, acc_ref, sems = rest[n_tables + 3 :]
    copies = []
    start = 0
    for i, source in enumerate(tables):
        count = source.shape[0]
        copies.append(pltpu.make_async_copy(source, table_ref.at[pl.ds(start, count)], sems.at[i]))
        start += count
    for copy in copies:
        copy.start()
    acc_ref[...] = jnp.zeros_like(acc_ref)
    total, width = own_ref.shape[1:]
    data_ref[:, :total, :] = own_ref[...].astype(F32)
    data_ref[:, total:, :] = par_ref[...].astype(F32)
    big = lax.broadcasted_iota(jnp.int32, (SLAB, width), 0).astype(F32).astype(BF16)
    wide = lax.broadcasted_iota(jnp.int32, (CB, width), 0).astype(F32).astype(BF16)
    small = lax.broadcasted_iota(jnp.int32, (UB, width), 0).astype(F32).astype(BF16)
    one, zero = jnp.ones((), BF16), jnp.zeros((), BF16)
    flip = ids[1]
    own_groups = (meta_own[4, 0] + UNROLL - 1) // UNROLL
    groups = own_groups + (meta_par[4, 0] + UNROLL - 1) // UNROLL
    for copy in copies:
        copy.wait()

    def group(g, _):
        is_own = g < own_groups
        tile = jnp.where(is_own, g, g - own_groups) * UNROLL
        first = pl.multiple_of(tile + jnp.where(is_own, 0, total), UNROLL)
        us, its, cs, vs = (data_ref[j, pl.ds(first, UNROLL), :] for j in range(4))

        def scalar(which, t):
            return jnp.where(is_own, meta_own[which, t], meta_par[which, t])

        for j in range(UNROLL):
            t = tile + j

            def row(x, height):
                return jnp.broadcast_to(x.astype(BF16), (height, width))

            items = its[j : j + 1, :] + scalar(3, t).astype(F32)
            pick_item = jnp.where(row(items, SLAB) == big, one, zero)
            pick_context = jnp.where(row(cs[j : j + 1, :], CB) == wide, one, zero)
            weight = jnp.where(row(us[j : j + 1, :], UB) == small, row(vs[j : j + 1, :], UB), zero)
            a = jnp.dot(table_ref[scalar(0, t)], pick_item, preferred_element_type=F32)
            b = jnp.dot(ctx_ref[scalar(1, t)], pick_context, preferred_element_type=F32)
            p = a * b
            hi = p.astype(BF16)
            lo = (p - hi.astype(F32)).astype(BF16)
            r = lax.dot_general(
                jnp.concatenate([weight, weight], 1),
                jnp.concatenate([hi, lo], 1),
                (((1,), (1,)), ((), ())),
                preferred_element_type=F32,
            )
            at = pl.ds(pl.multiple_of(scalar(2, t) ^ flip, UB), UB)
            acc_ref[at, :] += r
        return 0

    lax.fori_loop(0, groups, group, 0)
    start = 0
    for out in outs:
        out[...] = acc_ref[pl.ds(start, out.shape[0]), :]
        start += out.shape[0]


def swap(x, axis, distance):
    size = lax.axis_size(axis)
    return lax.ppermute(x, axis, [(i, i ^ distance) for i in range(size)])


def halves(size):
    steps = []
    while size > 1:
        size //= 2
        steps.append(size)
    return steps


def take_rows(x, start, count):
    return lax.dynamic_slice_in_dim(x, start, count, 0)


def item_order():
    items_size = lax.axis_size("items")
    top = items_size // 2
    order = halves(top) + [top]
    me = lax.axis_index("items")
    index = 0
    for distance in order:
        index = index * 2 + (me // distance) % 2
    return top, order, index


def scatter_items(x):
    top, order, index = item_order()
    me = lax.axis_index("items")
    for distance in order:
        half = x.shape[0] // 2
        bit = (me // distance) % 2
        keep = take_rows(x, bit * half, half)
        send = take_rows(x, (1 - bit) * half, half)
        x = keep + swap(send, "items", distance)
    return x


def joined(x, other, bit):
    return jnp.concatenate([jnp.where(bit == 0, x, other), jnp.where(bit == 0, other, x)], 0)


def gather_items(x):
    top, order, index = item_order()
    me = lax.axis_index("items")
    for distance in order[::-1]:
        x = joined(x, swap(x, "items", distance), (me // distance) % 2)
    return x


def sum_users(x):
    for distance in halves(lax.axis_size("users"))[::-1]:
        x = x + swap(x, "users", distance)
    return x


def scatter_users(x):
    size = lax.axis_size("users")
    me = lax.axis_index("users")
    for distance in halves(size)[::-1]:
        half = x.shape[0] // 2
        bit = (me // distance) % 2
        keep = take_rows(x, bit * half, half)
        x = keep + swap(take_rows(x, (1 - bit) * half, half), "users", distance)
    return x


def gather_users(x):
    size = lax.axis_size("users")
    me = lax.axis_index("users")
    for distance in halves(size):
        x = joined(x, swap(x, "users", distance), (me // distance) % 2)
    return x


def gather_table(item_factors):
    size = lax.axis_size("users")
    top, order, index = item_order()
    high = lax.axis_index("items") // top
    low = lax.axis_index("items") % top
    rows, width = item_factors.shape
    cols = width // 2
    if size > 16 or rows % (SLAB * top):
        mine = lax.dynamic_slice_in_dim(item_factors, high * cols, cols, 1)
        full = lax.all_gather(mine, "users", tiled=True)
        return [full.reshape(-1, SLAB, cols).transpose(0, 2, 1)], lambda slab, ids: slab
    count = rows // top
    mine = lax.dynamic_slice(item_factors, (low * count, high * cols), (count, cols))
    piece = mine.reshape(count // SLAB, SLAB, cols).transpose(0, 2, 1)
    steps = halves(size)
    steps = steps[:1] + steps[:0:-1]
    buffers = [piece]
    for n, distance in enumerate(steps):
        buffers = buffers + [swap(x, "users", distance) for x in buffers]
        if n == 0:
            buffers = [jnp.concatenate(buffers, 0)]
    for distance in halves(top)[::-1]:
        buffers = buffers + [swap(x, "items", distance) for x in buffers]
    held, part = rows // SLAB, count // SLAB

    def place(slab, ids):
        owner, inner = slab // held, slab % held
        far = owner ^ ids[0]
        position = sum((far // d % 2) * (1 << n) for n, d in enumerate(steps))
        return ((inner // part ^ ids[2]) * size + position) * part + inner % part

    return buffers, place


def local(
    tile_users,
    tile_owners,
    tile_blocks,
    tile_contexts,
    row_users,
    row_items,
    row_contexts,
    tile_values,
    tile_count,
    item_factors,
    context_factors,
    profile,
    feature_factors,
):
    top, order, index = item_order()
    items_size = lax.axis_size("items")
    high = lax.axis_index("items") // top
    low = lax.axis_index("items") % top
    tile_total = tile_users.shape[2]
    width = row_users.shape[3]
    rank_width = item_factors.shape[1]
    cols = rank_width // 2
    slab_users = profile.shape[0]
    user_rows = slab_users // items_size
    blocks_held = item_factors.shape[0] // IB
    ids = jnp.stack([lax.axis_index("users"), index * user_rows, low]).astype(jnp.int32)

    tables, place = gather_table(item_factors)
    contexts = lax.dynamic_slice_in_dim(context_factors, high * cols, cols, 1)
    contexts = contexts.reshape(-1, CB, cols).transpose(0, 2, 1)

    shape = (tile_total, width)
    meta, data = pl.pallas_call(
        lambda *refs: prep_kernel(place, blocks_held, *refs),
        out_shape=(
            jax.ShapeDtypeStruct((8, tile_total), jnp.int32),
            jax.ShapeDtypeStruct((4,) + shape, BF16),
        ),
        in_specs=[SM, SM] + [VM] * 8,
        out_specs=(VM, VM),
    )(
        ids,
        tile_count,
        tile_owners.reshape(tile_total, 1),
        tile_blocks.reshape(1, tile_total),
        tile_contexts.reshape(1, tile_total),
        tile_users.reshape(1, tile_total),
        row_users.reshape(shape),
        row_items.reshape(shape),
        row_contexts.reshape(shape),
        tile_values.reshape(shape),
    )
    meta_other = swap(meta, "items", top)
    data_other = swap(data, "items", top)

    rank_rows = rank_width // items_size
    item_part = sum_users(take_rows(gram(item_factors), index * rank_rows, rank_rows))
    context_part = take_rows(gram(context_factors), index * rank_rows, rank_rows)
    feature_part = scatter_items(gram(feature_factors))
    diagonal = (
        index * rank_rows + lax.broadcasted_iota(jnp.int32, item_part.shape, 0)
        == lax.broadcasted_iota(jnp.int32, item_part.shape, 1)
    ).astype(F32)
    normal = gather_items(item_part * context_part + feature_part + RIDGE * diagonal)
    normal_inverse = inverse(normal)

    dense = scatter_items(jnp.dot(profile, feature_factors, preferred_element_type=F32))

    sizes = (user_rows, user_rows, slab_users - 2 * user_rows)
    mine, near, away = pl.pallas_call(
        lambda *refs: tiles_kernel(len(tables), *refs),
        out_shape=tuple(jax.ShapeDtypeStruct((n, cols), F32) for n in sizes),
        in_specs=[SM, SM, SM, VM, VM, VM] + [ANY] * len(tables),
        out_specs=(VM, VM, VM),
        scratch_shapes=[
            pltpu.VMEM((sum(t.shape[0] for t in tables), cols, SLAB), BF16),
            pltpu.VMEM((4, 2 * tile_total, width), F32),
            pltpu.VMEM((slab_users, cols), F32),
            pltpu.SemaphoreType.DMA((len(tables),)),
        ],
    )(ids, meta, meta_other, data, data_other, contexts, *tables)
    sparse = jnp.concatenate([mine, near], 0)
    for distance in order[:-1]:
        half = away.shape[0] // 2
        came = swap(away, "items", distance)
        sparse = sparse + came
    mine, near = sparse[:user_rows], sparse[user_rows:]
    other = swap(near, "items", top)
    sparse = jnp.concatenate(
        [jnp.where(high == 0, mine, other), jnp.where(high == 0, other, mine)], 1
    )
    right_part = sparse + dense
    users_part = jnp.dot(right_part, normal_inverse, precision=HI).astype(BF16)

    user_gram = gather_items(sum_users(scatter_items(gram(users_part))))
    identity = jnp.eye(rank_width, dtype=F32)
    user_inverse = inverse(user_gram + RIDGE * identity)
    user_factors = gather_items(users_part)
    feature_terms = lax.dot_general(
        profile, user_factors, (((0,), (0,)), ((), ())), preferred_element_type=F32
    )
    feature_right = scatter_users(feature_terms)
    feature_part = jnp.dot(feature_right, user_inverse, precision=HI).astype(BF16)
    feature_new = gather_users(feature_part)
    return (user_factors, feature_new)


def solution(mesh):
    in_specs = (
        P("users", "items", None),
        P("users", "items", None, None),
        P("users", "items", None),
        P("users", "items", None),
        P("users", "items", None, None),
        P("users", "items", None, None),
        P("users", "items", None, None),
        P("users", "items", None, None),
        P("users", "items"),
        P("users", None),
        P(),
        P("users", "items"),
        P("items", None),
    )
    out_specs = (P("users", None), P("items", None))
    return jax.shard_map(local, mesh=mesh, in_specs=in_specs, out_specs=out_specs, check_vma=False)
```

```python
import jax
import jax.numpy as jnp
from jax import lax
from jax.experimental import pallas as pl
from jax.experimental.pallas import tpu as pltpu
from jax.sharding import PartitionSpec as P

CB = 128
IB = 16
UB = 16
SLAB = 128
RIDGE = 1.0
UNROLL = 32
FLOPS_US = 1000000000
PIVOTS = 8
HI = lax.Precision.HIGHEST
VM = pl.BlockSpec(memory_space=pltpu.VMEM)
SM = pl.BlockSpec(memory_space=pltpu.SMEM)
ANY = pl.BlockSpec(memory_space=pl.ANY)
F32 = jnp.float32
BF16 = jnp.bfloat16


def gram(matrix):
    return lax.dot_general(
        matrix, matrix, (((0,), (0,)), ((), ())), preferred_element_type=F32
    )


def mm(a, b, dims=(((1,), (0,)), ((), ()))):
    return lax.dot_general(a, b, dims, precision=HI, preferred_element_type=F32)


def solve_pivots(d, r):
    n = len(r)
    if n == 1:
        return [r[0] * (1.0 / d[0][0])]
    h = n // 2
    if n == 2:
        p = 1.0 / d[0][0]
        low = d[0][1] * p
        q = 1.0 / (d[1][1] - d[0][1] * low)
        last = (r[1] - low * r[0]) * q
        return [r[0] * p - low * last, last]
    first = [[d[i][j] if j >= i else None for j in range(h)] for i in range(h)]
    cross = [[d[i][h + j] for j in range(h)] for i in range(h)]
    t = solve_pivots(first, r[:h])
    w = [solve_pivots(first, [cross[i][j] for i in range(h)]) for j in range(h)]
    schur = [
        [
            d[h + i][h + j] - sum(cross[m][i] * w[j][m] for m in range(h)) if j >= i else None
            for j in range(h)
        ]
        for i in range(h)
    ]
    rest = [r[h + i] - sum(cross[m][i] * t[m] for m in range(h)) for i in range(h)]
    q = solve_pivots(schur, rest)
    return [t[m] - sum(w[j][m] * q[j] for j in range(h)) for m in range(h)] + q


def base_inverse(a):
    n = a.shape[0]
    lanes = lax.broadcasted_iota(jnp.int32, (PIVOTS, n), 1)
    lane1 = lax.broadcasted_iota(jnp.int32, (1, n), 1)
    blocks = [a[PIVOTS * i : PIVOTS * (i + 1), :] for i in range(n // PIVOTS)]

    def columns(block, k):
        return [jnp.broadcast_to(block[:, k + j : k + j + 1], (PIVOTS, n)) for j in range(PIVOTS)]

    for v in range(n // PIVOTS):
        k = v * PIVOTS
        pivot = columns(blocks[v], k)
        d = [[pivot[j][i : i + 1, :] for j in range(PIVOTS)] for i in range(PIVOTS)]
        inside = (lane1 >= k) & (lane1 < k + PIVOTS)
        r = [
            jnp.where(inside, (lane1 == k + i).astype(F32), blocks[v][i : i + 1, :])
            for i in range(PIVOTS)
        ]
        rows = [jnp.broadcast_to(x, (PIVOTS, n)) for x in solve_pivots(d, r)]
        inside = (lanes >= k) & (lanes < k + PIVOTS)
        new = []
        for i, block in enumerate(blocks):
            if i == v:
                sub = lax.broadcasted_iota(jnp.int32, (PIVOTS, n), 0)
                x = rows[0]
                for j in range(1, PIVOTS):
                    x = jnp.where(sub == j, rows[j], x)
            else:
                c = columns(block, k)
                x = jnp.where(inside, 0.0, block)
                u = c[0] * rows[0]
                for j in range(1, PIVOTS):
                    u = u + c[j] * rows[j]
                x = x - u
            new.append(x)
        blocks = new
    return jnp.concatenate(blocks, 0)


def inverse_value(a):
    n = a.shape[0]
    if n <= 128:
        return base_inverse(a)
    h = n // 2
    a12 = a[:h, h:]
    i11 = inverse_value(a[:h, :h])
    w = mm(i11, a12)
    i22 = inverse_value(a[h:, h:] - mm(a12, w, (((0,), (0,)), ((), ()))))
    nt = (((1,), (1,)), ((), ()))
    b12 = -mm(w, i22)
    b11 = i11 - mm(b12, w, nt)
    b21 = -mm(i22, w, nt)
    return jnp.concatenate(
        [jnp.concatenate([b11, b12], 1), jnp.concatenate([b21, i22], 1)], 0
    )


def inverse_kernel(ridge, *refs):
    index = kernel_ids(0)[3]
    parts, (out, full, sems) = refs[:-3], refs[-3:]
    copies = []
    for p, part in enumerate(parts):
        rows = part.shape[0]
        at = pl.ds(pl.multiple_of((p ^ index) * rows, rows), rows)
        copies.append(pltpu.make_async_copy(part, full.at[at], sems.at[p]))
    for copy in copies:
        copy.start()
    for copy in copies:
        copy.wait()
    a = full[...]
    if ridge:
        same = lax.broadcasted_iota(jnp.int32, a.shape, 0) == lax.broadcasted_iota(
            jnp.int32, a.shape, 1
        )
        a = a + jnp.where(same, RIDGE, 0.0)
    out[...] = inverse_value(a)


def inverse(parts, ridge):
    n = parts[0].shape[1]
    return pl.pallas_call(
        lambda *refs: inverse_kernel(ridge, *refs),
        out_shape=jax.ShapeDtypeStruct((n, n), F32),
        in_specs=[ANY] * len(parts),
        cost_estimate=cost(11),
        out_specs=VM,
        scratch_shapes=[pltpu.VMEM((n, n), F32), pltpu.SemaphoreType.DMA((len(parts),))],
    )(*parts)


def level_sizes(blocks):
    sizes = [1]
    while sum(sizes) < blocks:
        sizes.append(sum(sizes))
    return sizes


def dense_kernel(blocks, profile, features, *refs):
    ids = kernel_ids(0)
    outs, full = refs[:-1], refs[-1]
    f = features[...]
    full[...] = lax.dot_general(f, f, (((0,), (0,)), ((), ())), preferred_element_type=F32)
    rows, small = profile.shape[0] // blocks, full.shape[0] // blocks
    p = 0
    for out in outs:
        for i in range(out.shape[0] // (rows + small)):
            at = p ^ ids[3]
            start = i * (rows + small)
            out[start : start + rows, :] = jnp.dot(
                profile[pl.ds(pl.multiple_of(at * rows, rows), rows), :],
                f,
                preferred_element_type=F32,
            )
            out[start + rows : start + rows + small, :] = full[
                pl.ds(pl.multiple_of(at * small, small), small), :
            ]
            p += 1


def dense_parts(profile, features, blocks):
    n = features.shape[1]
    rows = profile.shape[0] // blocks + n // blocks
    return pl.pallas_call(
        lambda *refs: dense_kernel(blocks, *refs),
        out_shape=[jax.ShapeDtypeStruct((s * rows, n), F32) for s in level_sizes(blocks)],
        in_specs=[VM, VM],
        cost_estimate=cost(3.7),
        out_specs=[VM] * len(level_sizes(blocks)),
        scratch_shapes=[pltpu.VMEM((n, n), F32)],
    )(profile, features)


def solve_kernel(blocks, mine, other, dense, inverse_ref, users_out, *refs):
    outs, full = refs[:-1], refs[-1]
    ids = kernel_ids(0)
    rows = mine.shape[0]
    first = ids[4] == 0
    left = jnp.where(first, mine[...], other[...])
    right = jnp.where(first, other[...], mine[...])
    total = jnp.concatenate([left, right], 1) + dense[:rows, :]
    users = mm(total, inverse_ref[...]).astype(BF16)
    users_out[...] = users
    full[...] = lax.dot_general(
        users, users, (((0,), (0,)), ((), ())), preferred_element_type=F32
    )
    small = full.shape[0] // blocks
    p = 0
    for out in outs:
        for i in range(out.shape[0] // small):
            at = pl.ds(pl.multiple_of((p ^ ids[3]) * small, small), small)
            out[i * small : (i + 1) * small, :] = full[at, :]
            p += 1


def solve_users(mine, other, dense, normal_inverse, blocks):
    n = normal_inverse.shape[0]
    sizes = level_sizes(blocks)
    return pl.pallas_call(
        lambda *refs: solve_kernel(blocks, *refs),
        out_shape=[jax.ShapeDtypeStruct((mine.shape[0], n), BF16)]
        + [jax.ShapeDtypeStruct((s * (n // blocks), n), F32) for s in sizes],
        in_specs=[VM, VM, VM, VM],
        cost_estimate=cost(3),
        out_specs=[VM] * (1 + len(sizes)),
        scratch_shapes=[pltpu.VMEM((n, n), F32)],
    )(mine, other, dense, normal_inverse)


def kernel_ids(unit):
    top, order, index = item_order()
    me = lax.axis_index("items")
    return lax.axis_index("users"), index * unit, me % top, index, me // top


def cost(microseconds):
    return pl.CostEstimate(
        flops=int(microseconds * FLOPS_US), bytes_accessed=0, transcendentals=0
    )


def prep_kernel(place, blocks_held, count, owners, blocks, contexts, users, ru, ri, rc, val, meta, data):
    ids = kernel_ids(0)
    tiles_here, width = ru.shape
    shape = (tiles_here, tiles_here)
    eye = lax.broadcasted_iota(jnp.int32, shape, 0) == lax.broadcasted_iota(jnp.int32, shape, 1)
    owner = jnp.sum(jnp.where(eye, owners[...], 0), axis=0, keepdims=True)
    per_slab = SLAB // IB
    block = owner * blocks_held + blocks[...]
    rows = [
        place(block // per_slab, ids),
        contexts[...],
        users[...] * UB,
        block % per_slab * IB,
        jnp.full((1, tiles_here), count[0, 0], jnp.int32),
    ]
    for i, row in enumerate(rows):
        meta[i : i + 1, :] = row
    meta[len(rows) :, :] = jnp.zeros((8 - len(rows), tiles_here), jnp.int32)
    alive = lax.broadcasted_iota(jnp.int32, (tiles_here, width), 0) < count[0, 0]
    data[0] = ru[...].astype(F32).astype(BF16)
    data[1] = ri[...].astype(F32).astype(BF16)
    data[2] = rc[...].astype(F32).astype(BF16)
    data[3] = jnp.where(alive, val[...].astype(F32), 0.0).astype(BF16)


def tiles_kernel(n_tables, unit, meta_hbm, meta_par_hbm, own_hbm, par_hbm, ctx_hbm, *rest):
    tables = rest[:n_tables]
    outs = rest[n_tables:-8]
    table_ref, raw_ref, ctx_ref, data_ref, acc_ref, meta_own, meta_par, sems = rest[-8:]
    total, width = own_hbm.shape[1:]
    copies = [
        pltpu.make_async_copy(own_hbm, raw_ref.at[0], sems.at[0]),
        pltpu.make_async_copy(par_hbm, raw_ref.at[1], sems.at[1]),
        pltpu.make_async_copy(meta_hbm, meta_own, sems.at[2]),
        pltpu.make_async_copy(meta_par_hbm, meta_par, sems.at[3]),
        pltpu.make_async_copy(ctx_hbm, ctx_ref, sems.at[4]),
    ]
    start = 0
    for i, source in enumerate(tables):
        count = source.shape[0]
        copies.append(
            pltpu.make_async_copy(source, table_ref.at[pl.ds(start, count)], sems.at[5 + i])
        )
        start += count
    for copy in copies:
        copy.start()
    acc_ref[...] = jnp.zeros_like(acc_ref)
    copies[0].wait()
    data_ref[:, :total, :] = raw_ref[0].astype(F32)
    copies[1].wait()
    data_ref[:, total:, :] = raw_ref[1].astype(F32)
    big = lax.broadcasted_iota(jnp.int32, (SLAB, width), 0).astype(F32).astype(BF16)
    wide = lax.broadcasted_iota(jnp.int32, (CB, width), 0).astype(F32).astype(BF16)
    small = lax.broadcasted_iota(jnp.int32, (UB, width), 0).astype(F32).astype(BF16)
    one, zero = jnp.ones((), BF16), jnp.zeros((), BF16)
    flip = kernel_ids(unit)[1]
    copies[2].wait()
    copies[3].wait()
    own_groups = (meta_own[4, 0] + UNROLL - 1) // UNROLL
    groups = own_groups + (meta_par[4, 0] + UNROLL - 1) // UNROLL
    for copy in copies[4:]:
        copy.wait()

    def group(g, _):
        is_own = g < own_groups
        tile = jnp.where(is_own, g, g - own_groups) * UNROLL
        first = pl.multiple_of(tile + jnp.where(is_own, 0, total), UNROLL)
        us, its, cs, vs = (data_ref[j, pl.ds(first, UNROLL), :] for j in range(4))

        def scalar(which, t):
            return jnp.where(is_own, meta_own[which, t], meta_par[which, t])

        for j in range(UNROLL):
            t = tile + j

            def row(x, height):
                return jnp.broadcast_to(x.astype(BF16), (height, width))

            items = its[j : j + 1, :] + scalar(3, t).astype(F32)
            pick_item = jnp.where(row(items, SLAB) == big, one, zero)
            pick_context = jnp.where(row(cs[j : j + 1, :], CB) == wide, one, zero)
            weight = jnp.where(row(us[j : j + 1, :], UB) == small, row(vs[j : j + 1, :], UB), zero)
            a = jnp.dot(table_ref[scalar(0, t)], pick_item, preferred_element_type=F32)
            b = jnp.dot(ctx_ref[scalar(1, t)], pick_context, preferred_element_type=F32)
            p = a * b
            hi = p.astype(BF16)
            lo = (p - hi.astype(F32)).astype(BF16)
            r = lax.dot_general(
                jnp.concatenate([weight, weight], 1),
                jnp.concatenate([hi, lo], 1),
                (((1,), (1,)), ((), ())),
                preferred_element_type=F32,
            )
            at = pl.ds(pl.multiple_of(scalar(2, t) ^ flip, UB), UB)
            acc_ref[at, :] += r
        return 0

    lax.fori_loop(0, groups, group, 0)
    start = 0
    for out in outs:
        out[...] = acc_ref[pl.ds(start, out.shape[0]), :]
        start += out.shape[0]


def swap(x, axis, distance):
    size = lax.axis_size(axis)
    return lax.ppermute(x, axis, [(i, i ^ distance) for i in range(size)])


def halves(size):
    steps = []
    while size > 1:
        size //= 2
        steps.append(size)
    return steps


def take_rows(x, start, count):
    return lax.dynamic_slice_in_dim(x, start, count, 0)


def item_order():
    items_size = lax.axis_size("items")
    top = items_size // 2
    order = halves(top) + [top]
    me = lax.axis_index("items")
    index = 0
    for distance in order:
        index = index * 2 + (me // distance) % 2
    return top, order, index


def after(x, earlier):
    return lax.optimization_barrier((x, earlier))[0]


def scatter_levels(levels, order):
    for distance in order:
        came = swap(levels[-1], "items", distance)
        start, kept = 0, []
        for x in levels[:-1]:
            kept.append(x + came[start : start + x.shape[0]])
            start += x.shape[0]
        levels = kept
    return levels


def joined(x, other, bit):
    return jnp.concatenate([jnp.where(bit == 0, x, other), jnp.where(bit == 0, other, x)], 0)


def gather_users(x):
    size = lax.axis_size("users")
    me = lax.axis_index("users")
    for distance in halves(size):
        x = joined(x, swap(x, "users", distance), (me // distance) % 2)
    return x


def table_layout(item_factors):
    size = lax.axis_size("users")
    top, order, index = item_order()
    high = lax.axis_index("items") // top
    low = lax.axis_index("items") % top
    rows, width = item_factors.shape
    cols = width // 2
    if size > 16 or rows % (SLAB * top):
        mine = lax.dynamic_slice_in_dim(item_factors, high * cols, cols, 1)
        return mine, None, lambda slab, ids: slab
    count = rows // top
    mine = lax.dynamic_slice(item_factors, (low * count, high * cols), (count, cols))
    piece = mine.reshape(count // SLAB, SLAB, cols).transpose(0, 2, 1)
    steps = halves(size)
    steps = steps[:1] + steps[:0:-1]
    held, part = rows // SLAB, count // SLAB

    def place(slab, ids):
        owner, inner = slab // held, slab % held
        far = owner ^ ids[0]
        position = sum((far // d % 2) * (1 << n) for n, d in enumerate(steps))
        return ((inner // part ^ ids[2]) * size + position) * part + inner % part

    return piece, steps, place


def local(
    tile_users,
    tile_owners,
    tile_blocks,
    tile_contexts,
    row_users,
    row_items,
    row_contexts,
    tile_values,
    tile_count,
    item_factors,
    context_factors,
    profile,
    feature_factors,
):
    top, order, index = item_order()
    items_size = lax.axis_size("items")
    high = lax.axis_index("items") // top
    low = lax.axis_index("items") % top
    tile_total = tile_users.shape[2]
    width = row_users.shape[3]
    rank_width = item_factors.shape[1]
    cols = rank_width // 2
    slab_users = profile.shape[0]
    user_rows = slab_users // items_size
    blocks_held = item_factors.shape[0] // IB
    piece, steps, place = table_layout(item_factors)
    if steps:
        came = swap(piece, "users", steps[0])

    shape = (tile_total, width)
    meta, data = pl.pallas_call(
        lambda *refs: prep_kernel(place, blocks_held, *refs),
        out_shape=(
            jax.ShapeDtypeStruct((8, tile_total), jnp.int32),
            jax.ShapeDtypeStruct((4,) + shape, BF16),
        ),
        in_specs=[SM] + [VM] * 8,
        out_specs=(VM, VM),
        cost_estimate=cost(1.7),
    )(
        after(tile_count, piece),
        tile_owners.reshape(tile_total, 1),
        tile_blocks.reshape(1, tile_total),
        tile_contexts.reshape(1, tile_total),
        tile_users.reshape(1, tile_total),
        row_users.reshape(shape),
        row_items.reshape(shape),
        row_contexts.reshape(shape),
        tile_values.reshape(shape),
    )
    meta_other = swap(meta, "items", top)
    data_other = swap(data, "items", top)

    rank_rows = rank_width // items_size
    item_part = take_rows(gram(after(item_factors, data)), index * rank_rows, rank_rows)
    user_steps = halves(lax.axis_size("users"))[::-1]
    item_other = swap(item_part, "users", user_steps[0])

    if steps:
        tables = [jnp.concatenate([piece, after(came, item_part)], 0)]
        tables = tables + [swap(tables[0], "users", d) for d in steps[1:2]]
        early = [swap(tables[0], "users", d) for d in steps[2:3]]
        ready = tables[0]
    else:
        full = lax.all_gather(piece, "users", tiled=True)
        tables, early = [full.reshape(-1, SLAB, cols).transpose(0, 2, 1)], []
        ready = piece
    levels = dense_parts(after(profile, ready), feature_factors, items_size)
    item_part = item_part + after(item_other, levels[0])
    pending = [swap(item_part, "users", d) for d in user_steps[1:2]]
    late = after(context_factors, item_part)
    contexts = lax.dynamic_slice_in_dim(late, high * cols, cols, 1)
    contexts = contexts.reshape(-1, CB, cols).transpose(0, 2, 1)
    context_part = take_rows(gram(late), index * rank_rows, rank_rows)
    levels = scatter_levels(levels, order[:-1])
    dense_other = swap(levels[1], "items", top)
    if early:
        tables[1] = after(tables[1], (levels[1], contexts, context_part))
        tables = tables + early + [swap(tables[1], "users", steps[2])]
    for n, distance in enumerate(user_steps[1:]):
        other = pending[0] if n == 0 else swap(item_part, "users", distance)
        item_part = item_part + after(other, tables[1] if n == 0 and early else other)
    if steps:
        for distance in halves(top)[::-1]:
            tables = tables + [swap(x, "items", distance) for x in tables]
    dense = levels[0] + after(dense_other, item_part)
    diagonal = (
        index * rank_rows + lax.broadcasted_iota(jnp.int32, item_part.shape, 0)
        == lax.broadcasted_iota(jnp.int32, item_part.shape, 1)
    ).astype(F32)
    normal = [item_part * context_part + dense[user_rows:] + RIDGE * diagonal]
    data_other = after(data_other, normal[0])
    normal = normal + [swap(normal[0], "items", top)]

    sizes = [s * user_rows for s in level_sizes(items_size)]
    levels = pl.pallas_call(
        lambda *refs: tiles_kernel(len(tables), user_rows, *refs),
        out_shape=[jax.ShapeDtypeStruct((n, cols), F32) for n in sizes],
        in_specs=[ANY] * (5 + len(tables)),
        cost_estimate=cost(15),
        out_specs=[VM] * len(sizes),
        scratch_shapes=[
            pltpu.VMEM((sum(t.shape[0] for t in tables), cols, SLAB), BF16),
            pltpu.VMEM((2,) + data.shape, BF16),
            pltpu.VMEM(contexts.shape, BF16),
            pltpu.VMEM((4, 2 * tile_total, width), F32),
            pltpu.VMEM((slab_users, cols), F32),
            pltpu.SMEM(meta.shape, jnp.int32),
            pltpu.SMEM(meta.shape, jnp.int32),
            pltpu.SemaphoreType.DMA((5 + len(tables),)),
        ],
    )(meta, meta_other, data, data_other, contexts, *tables)
    mine, near = scatter_levels(levels, order[:-1])
    other = swap(near, "items", top)
    normal[1] = after(normal[1], levels[0])
    for distance in order[-2::-1]:
        normal = normal + [swap(x, "items", distance) for x in normal]
    normal[0] = after(normal[0], near)
    normal_inverse = inverse(normal, False)
    users_part, *levels = solve_users(mine, other, dense, normal_inverse, items_size)

    levels = scatter_levels(levels, order[:-1])
    users_sent = after(users_part, levels[1])
    users_other = swap(users_sent, "items", top)
    (part,) = scatter_levels(levels, order[-1:])
    sums = [part]
    for distance in user_steps:
        part = part + swap(part, "users", distance)
        sums.append(part)
    users_other = after(users_other, sums[1])
    user_factors = joined(users_part, users_other, high)
    for distance in order[-2::-1]:
        bit = (lax.axis_index("items") // distance) % 2
        user_factors = joined(user_factors, swap(user_factors, "items", distance), bit)
    feature_right = lax.dot_general(
        profile,
        after(user_factors, sums[2 % len(sums)]),
        (((0,), (0,)), ((), ())),
        preferred_element_type=F32,
    )
    users_me = lax.axis_index("users")
    sends = []
    gathered = [part]
    for n, distance in enumerate(order[::-1]):
        gathered = gathered + [swap(x, "items", distance) for x in gathered]
    for n, distance in enumerate(user_steps):
        half = feature_right.shape[0] // 2
        bit = (users_me // distance) % 2
        keep = take_rows(feature_right, bit * half, half)
        send = take_rows(feature_right, (1 - bit) * half, half)
        sends.append(send)
        feature_right = keep + swap(send, "users", distance)
    gathered = [after(gathered[0], sends[-1])] + gathered[1:]
    user_inverse = inverse(gathered, True)
    feature_part = jnp.dot(feature_right, user_inverse, precision=HI).astype(BF16)
    feature_new = gather_users(feature_part)
    return (user_factors, feature_new)


def solution(mesh):
    in_specs = (
        P("users", "items", None),
        P("users", "items", None, None),
        P("users", "items", None),
        P("users", "items", None),
        P("users", "items", None, None),
        P("users", "items", None, None),
        P("users", "items", None, None),
        P("users", "items", None, None),
        P("users", "items"),
        P("users", None),
        P(),
        P("users", "items"),
        P("items", None),
    )
    out_specs = (P("users", None), P("items", None))
    return jax.shard_map(local, mesh=mesh, in_specs=in_specs, out_specs=out_specs, check_vma=False)
```

```python
import jax
import jax.numpy as jnp
from jax import lax
from jax.experimental import pallas as pl
from jax.experimental.pallas import tpu as pltpu
from jax.sharding import PartitionSpec as P

CB = 128
IB = 16
UB = 16
SLAB = 128
RIDGE = 1.0
UNROLL = 32
FLOPS_US = 1000000000
VMEM_GRANT = 16 << 20
PIVOTS = 8
HI = lax.Precision.HIGHEST
VM = pl.BlockSpec(memory_space=pltpu.VMEM)
SM = pl.BlockSpec(memory_space=pltpu.SMEM)
ANY = pl.BlockSpec(memory_space=pl.ANY)
HBM = pl.BlockSpec(memory_space=pltpu.HBM)
F32 = jnp.float32
BF16 = jnp.bfloat16


def gram(matrix):
    return lax.dot_general(
        matrix, matrix, (((0,), (0,)), ((), ())), preferred_element_type=F32
    )


def mm(a, b, dims=(((1,), (0,)), ((), ()))):
    return lax.dot_general(a, b, dims, precision=HI, preferred_element_type=F32)


def solve_pivots(d, r):
    n = len(r)
    if n == 1:
        return [r[0] * (1.0 / d[0][0])]
    h = n // 2
    if n == 2:
        p = 1.0 / d[0][0]
        low = d[0][1] * p
        q = 1.0 / (d[1][1] - d[0][1] * low)
        last = (r[1] - low * r[0]) * q
        return [r[0] * p - low * last, last]
    first = [[d[i][j] if j >= i else None for j in range(h)] for i in range(h)]
    cross = [[d[i][h + j] for j in range(h)] for i in range(h)]
    t = solve_pivots(first, r[:h])
    w = [solve_pivots(first, [cross[i][j] for i in range(h)]) for j in range(h)]
    schur = [
        [
            d[h + i][h + j] - sum(cross[m][i] * w[j][m] for m in range(h)) if j >= i else None
            for j in range(h)
        ]
        for i in range(h)
    ]
    rest = [r[h + i] - sum(cross[m][i] * t[m] for m in range(h)) for i in range(h)]
    q = solve_pivots(schur, rest)
    return [t[m] - sum(w[j][m] * q[j] for j in range(h)) for m in range(h)] + q


def base_inverse(a):
    n = a.shape[0]
    lanes = lax.broadcasted_iota(jnp.int32, (PIVOTS, n), 1)
    lane1 = lax.broadcasted_iota(jnp.int32, (1, n), 1)
    blocks = [a[PIVOTS * i : PIVOTS * (i + 1), :] for i in range(n // PIVOTS)]

    def columns(block, k):
        return [jnp.broadcast_to(block[:, k + j : k + j + 1], (PIVOTS, n)) for j in range(PIVOTS)]

    for v in range(n // PIVOTS):
        k = v * PIVOTS
        pivot = columns(blocks[v], k)
        d = [[pivot[j][i : i + 1, :] for j in range(PIVOTS)] for i in range(PIVOTS)]
        inside = (lane1 >= k) & (lane1 < k + PIVOTS)
        r = [
            jnp.where(inside, (lane1 == k + i).astype(F32), blocks[v][i : i + 1, :])
            for i in range(PIVOTS)
        ]
        rows = [jnp.broadcast_to(x, (PIVOTS, n)) for x in solve_pivots(d, r)]
        inside = (lanes >= k) & (lanes < k + PIVOTS)
        new = []
        for i, block in enumerate(blocks):
            if i == v:
                sub = lax.broadcasted_iota(jnp.int32, (PIVOTS, n), 0)
                x = rows[0]
                for j in range(1, PIVOTS):
                    x = jnp.where(sub == j, rows[j], x)
            else:
                c = columns(block, k)
                x = jnp.where(inside, 0.0, block)
                u = c[0] * rows[0]
                for j in range(1, PIVOTS):
                    u = u + c[j] * rows[j]
                x = x - u
            new.append(x)
        blocks = new
    return jnp.concatenate(blocks, 0)


def inverse_value(a):
    n = a.shape[0]
    if n <= 128:
        return base_inverse(a)
    h = n // 2
    a12 = a[:h, h:]
    i11 = inverse_value(a[:h, :h])
    w = mm(i11, a12)
    i22 = inverse_value(a[h:, h:] - mm(a12, w, (((0,), (0,)), ((), ()))))
    nt = (((1,), (1,)), ((), ()))
    b12 = -mm(w, i22)
    b11 = i11 - mm(b12, w, nt)
    b21 = -mm(i22, w, nt)
    return jnp.concatenate(
        [jnp.concatenate([b11, b12], 1), jnp.concatenate([b21, i22], 1)], 0
    )


def inverse_kernel(ridge, *refs):
    parts, out, full = refs[:-2], refs[-2], refs[-1]
    index = kernel_ids(0)[3]
    for p, part in enumerate(parts):
        rows = part.shape[0]
        full[pl.ds(pl.multiple_of((p ^ index) * rows, rows), rows), :] = part[...]
    a = full[...]
    if ridge:
        same = lax.broadcasted_iota(jnp.int32, a.shape, 0) == lax.broadcasted_iota(
            jnp.int32, a.shape, 1
        )
        a = a + jnp.where(same, RIDGE, 0.0)
    out[...] = inverse_value(a)


def inverse(parts, ridge):
    n = parts[0].shape[1]
    return pl.pallas_call(
        lambda *refs: inverse_kernel(ridge, *refs),
        out_shape=pltpu.VMEM((n, n), F32),
        in_specs=[VM] * len(parts),
        out_specs=VM,
        cost_estimate=cost(11),
    compiler_params=pltpu.CompilerParams(vmem_limit_bytes=VMEM_GRANT),
        scratch_shapes=[pltpu.VMEM((n, n), F32)],
    )(*here(*parts))


def level_sizes(blocks):
    sizes = [1]
    while sum(sizes) < blocks:
        sizes.append(sum(sizes))
    return sizes


def dense_kernel(blocks, profile, features, *refs):
    ids = kernel_ids(0)
    outs, full = refs[:-1], refs[-1]
    f = features[...]
    full[...] = lax.dot_general(f, f, (((0,), (0,)), ((), ())), preferred_element_type=F32)
    rows, small = profile.shape[0] // blocks, full.shape[0] // blocks
    p = 0
    for out in outs:
        for i in range(out.shape[0] // (rows + small)):
            at = p ^ ids[3]
            start = i * (rows + small)
            out[start : start + rows, :] = jnp.dot(
                profile[pl.ds(pl.multiple_of(at * rows, rows), rows), :],
                f,
                preferred_element_type=F32,
            )
            out[start + rows : start + rows + small, :] = full[
                pl.ds(pl.multiple_of(at * small, small), small), :
            ]
            p += 1


def dense_parts(profile, features, blocks):
    n = features.shape[1]
    rows = profile.shape[0] // blocks + n // blocks
    return pl.pallas_call(
        lambda *refs: dense_kernel(blocks, *refs),
        out_shape=[pltpu.VMEM((s * rows, n), F32) for s in level_sizes(blocks)],
        in_specs=[VM, VM],
        cost_estimate=cost(3.7),
        compiler_params=pltpu.CompilerParams(vmem_limit_bytes=VMEM_GRANT),
        out_specs=[VM] * len(level_sizes(blocks)),
        scratch_shapes=[pltpu.VMEM((n, n), F32)],
    )(*here(profile, features))


def solve_kernel(blocks, mine, other, dense, inverse_ref, users_out, *refs):
    outs, full = refs[:-1], refs[-1]
    ids = kernel_ids(0)
    rows = mine.shape[0]
    first = ids[4] == 0
    left = jnp.where(first, mine[...], other[...])
    right = jnp.where(first, other[...], mine[...])
    total = jnp.concatenate([left, right], 1) + dense[:rows, :]
    users = mm(total, inverse_ref[...]).astype(BF16)
    users_out[...] = users
    full[...] = lax.dot_general(
        users, users, (((0,), (0,)), ((), ())), preferred_element_type=F32
    )
    small = full.shape[0] // blocks
    p = 0
    for out in outs:
        for i in range(out.shape[0] // small):
            at = pl.ds(pl.multiple_of((p ^ ids[3]) * small, small), small)
            out[i * small : (i + 1) * small, :] = full[at, :]
            p += 1


def solve_users(mine, other, dense, normal_inverse, blocks):
    n = normal_inverse.shape[0]
    sizes = level_sizes(blocks)
    return pl.pallas_call(
        lambda *refs: solve_kernel(blocks, *refs),
        out_shape=[pltpu.VMEM((mine.shape[0], n), BF16)]
        + [pltpu.VMEM((s * (n // blocks), n), F32) for s in sizes],
        in_specs=[VM, VM, VM, VM],
        cost_estimate=cost(3),
        compiler_params=pltpu.CompilerParams(vmem_limit_bytes=VMEM_GRANT),
        out_specs=[VM] * (1 + len(sizes)),
        scratch_shapes=[pltpu.VMEM((n, n), F32)],
    )(*here(mine, other, dense, normal_inverse))


def kernel_ids(unit):
    top, _, index = item_order()
    me = lax.axis_index("items")
    return lax.axis_index("users"), index * unit, me % top, index, me // top


def here(*arrays):
    return [pltpu.with_memory_space_constraint(x, pltpu.VMEM) for x in arrays]


def cost(microseconds):
    return pl.CostEstimate(
        flops=int(microseconds * FLOPS_US), bytes_accessed=0, transcendentals=0
    )


def prep_kernel(place, blocks_held, count, *refs):
    inputs, (meta, data), scratch, sems = refs[:8], refs[8:10], refs[10:18], refs[18]
    copies = [
        pltpu.make_async_copy(source, target, sems.at[i])
        for i, (source, target) in enumerate(zip(inputs, scratch))
    ]
    for copy in copies:
        copy.start()
    owners, blocks, contexts, users, ru, ri, rc, val = scratch
    ids = kernel_ids(0)
    tiles_here, width = ru.shape
    for copy in copies:
        copy.wait()
    per_slab = SLAB // IB
    block = owners[...] * blocks_held + blocks[...]
    rows = [
        place(block // per_slab, ids),
        contexts[...],
        users[...] * UB,
        block % per_slab * IB,
        jnp.full((1, tiles_here), count[0, 0], jnp.int32),
    ]
    for i, row in enumerate(rows):
        meta[i : i + 1, :] = row
    meta[len(rows) :, :] = jnp.zeros((8 - len(rows), tiles_here), jnp.int32)
    alive = lax.broadcasted_iota(jnp.int32, (tiles_here, width), 0) < count[0, 0]
    data[0] = ru[...].astype(F32).astype(BF16)
    data[1] = ri[...].astype(F32).astype(BF16)
    data[2] = rc[...].astype(F32).astype(BF16)
    data[3] = jnp.where(alive, val[...].astype(F32), 0.0).astype(BF16)


def tiles_kernel(n_tables, unit, meta_hbm, meta_par_hbm, own_hbm, par_hbm, ctx_hbm, *rest):
    tables = rest[:n_tables]
    outs = rest[n_tables:-8]
    table_ref, raw_ref, ctx_ref, data_ref, acc_ref, meta_own, meta_par, sems = rest[-8:]
    total, width = own_hbm.shape[1:]
    copies = [
        pltpu.make_async_copy(own_hbm, raw_ref.at[0], sems.at[0]),
        pltpu.make_async_copy(par_hbm, raw_ref.at[1], sems.at[1]),
        pltpu.make_async_copy(meta_hbm, meta_own, sems.at[2]),
        pltpu.make_async_copy(meta_par_hbm, meta_par, sems.at[3]),
        pltpu.make_async_copy(ctx_hbm, ctx_ref, sems.at[4]),
    ]
    start = 0
    for i, source in enumerate(tables):
        count = source.shape[0]
        copies.append(
            pltpu.make_async_copy(source, table_ref.at[pl.ds(start, count)], sems.at[5 + i])
        )
        start += count
    for copy in copies:
        copy.start()
    acc_ref[...] = jnp.zeros_like(acc_ref)
    copies[0].wait()
    data_ref[:, :total, :] = raw_ref[0].astype(F32)
    copies[1].wait()
    data_ref[:, total:, :] = raw_ref[1].astype(F32)
    big = lax.broadcasted_iota(jnp.int32, (SLAB, width), 0).astype(F32).astype(BF16)
    wide = lax.broadcasted_iota(jnp.int32, (CB, width), 0).astype(F32).astype(BF16)
    small = lax.broadcasted_iota(jnp.int32, (UB, width), 0).astype(F32).astype(BF16)
    one, zero = jnp.ones((), BF16), jnp.zeros((), BF16)
    flip = kernel_ids(unit)[1]
    copies[2].wait()
    copies[3].wait()
    own_groups = (meta_own[4, 0] + UNROLL - 1) // UNROLL
    groups = own_groups + (meta_par[4, 0] + UNROLL - 1) // UNROLL
    for copy in copies[4:]:
        copy.wait()

    def group(g, _):
        is_own = g < own_groups
        tile = jnp.where(is_own, g, g - own_groups) * UNROLL
        first = pl.multiple_of(tile + jnp.where(is_own, 0, total), UNROLL)
        us, its, cs, vs = (data_ref[j, pl.ds(first, UNROLL), :] for j in range(4))

        def scalar(which, t):
            return jnp.where(is_own, meta_own[which, t], meta_par[which, t])

        for j in range(UNROLL):
            t = tile + j

            def row(x, height):
                return jnp.broadcast_to(x.astype(BF16), (height, width))

            items = its[j : j + 1, :] + scalar(3, t).astype(F32)
            pick_item = jnp.where(row(items, SLAB) == big, one, zero)
            pick_context = jnp.where(row(cs[j : j + 1, :], CB) == wide, one, zero)
            weight = jnp.where(row(us[j : j + 1, :], UB) == small, row(vs[j : j + 1, :], UB), zero)
            a = jnp.dot(table_ref[scalar(0, t)], pick_item, preferred_element_type=F32)
            b = jnp.dot(ctx_ref[scalar(1, t)], pick_context, preferred_element_type=F32)
            p = a * b
            hi = p.astype(BF16)
            lo = (p - hi.astype(F32)).astype(BF16)
            r = lax.dot_general(
                jnp.concatenate([weight, weight], 1),
                jnp.concatenate([hi, lo], 1),
                (((1,), (1,)), ((), ())),
                preferred_element_type=F32,
            )
            at = pl.ds(pl.multiple_of(scalar(2, t) ^ flip, UB), UB)
            acc_ref[at, :] += r
        return 0

    lax.fori_loop(0, groups, group, 0)
    start = 0
    for out in outs:
        out[...] = acc_ref[pl.ds(start, out.shape[0]), :]
        start += out.shape[0]


def swap(x, axis, distance):
    size = lax.axis_size(axis)
    return lax.ppermute(x, axis, [(i, i ^ distance) for i in range(size)])


def halves(size):
    steps = []
    while size > 1:
        size //= 2
        steps.append(size)
    return steps


def take_rows(x, start, count):
    return lax.dynamic_slice_in_dim(x, start, count, 0)


def item_order():
    items_size = lax.axis_size("items")
    top = items_size // 2
    order = halves(top) + [top]
    me = lax.axis_index("items")
    index = 0
    for distance in order:
        index = index * 2 + (me // distance) % 2
    return top, order, index


def after(x, earlier):
    return lax.optimization_barrier((x, earlier))[0]


def scatter_levels(levels, order):
    for distance in order:
        came = swap(levels[-1], "items", distance)
        start, kept = 0, []
        for x in levels[:-1]:
            kept.append(x + came[start : start + x.shape[0]])
            start += x.shape[0]
        levels = kept
    return levels


def joined(x, other, bit):
    return jnp.concatenate([jnp.where(bit == 0, x, other), jnp.where(bit == 0, other, x)], 0)


def gather_users(x, steps):
    me = lax.axis_index("users")
    for distance in steps[::-1]:
        x = joined(x, swap(x, "users", distance), (me // distance) % 2)
    return x


def table_layout(item_factors):
    size = lax.axis_size("users")
    top, _, _ = item_order()
    high = lax.axis_index("items") // top
    low = lax.axis_index("items") % top
    rows, width = item_factors.shape
    cols = width // 2
    if size > 16 or rows % (SLAB * top):
        mine = lax.dynamic_slice_in_dim(item_factors, high * cols, cols, 1)
        return mine, None, lambda slab, ids: slab
    count = rows // top
    mine = lax.dynamic_slice(item_factors, (low * count, high * cols), (count, cols))
    piece = mine.reshape(count // SLAB, SLAB, cols).transpose(0, 2, 1)
    steps = halves(size)
    steps = steps[:1] + steps[:0:-1]
    held, part = rows // SLAB, count // SLAB

    def place(slab, ids):
        owner, inner = slab // held, slab % held
        far = owner ^ ids[0]
        position = sum((far // d % 2) * (1 << n) for n, d in enumerate(steps))
        return ((inner // part ^ ids[2]) * size + position) * part + inner % part

    return piece, steps, place


def local(
    tile_users,
    tile_owners,
    tile_blocks,
    tile_contexts,
    row_users,
    row_items,
    row_contexts,
    tile_values,
    tile_count,
    item_factors,
    context_factors,
    profile,
    feature_factors,
):
    top, order, index = item_order()
    items_size = lax.axis_size("items")
    high = lax.axis_index("items") // top
    tile_total = tile_users.shape[2]
    width = row_users.shape[3]
    rank_width = item_factors.shape[1]
    cols = rank_width // 2
    slab_users = profile.shape[0]
    user_rows = slab_users // items_size
    blocks_held = item_factors.shape[0] // IB
    piece, steps, place = table_layout(item_factors)
    shape = (tile_total, width)
    meta, data = pl.pallas_call(
        lambda *refs: prep_kernel(place, blocks_held, *refs),
        out_shape=(
            pltpu.VMEM((8, tile_total), jnp.int32),
            pltpu.VMEM((4,) + shape, BF16),
        ),
        in_specs=[SM] + [HBM] * 8,
        out_specs=(VM, VM),
        cost_estimate=cost(1.7),
        compiler_params=pltpu.CompilerParams(vmem_limit_bytes=VMEM_GRANT),
        scratch_shapes=[
            *[pltpu.VMEM((1, tile_total), jnp.int32)] * 4,
            *[pltpu.VMEM(shape, jnp.int32)] * 3,
            pltpu.VMEM(shape, BF16),
            pltpu.SemaphoreType.DMA((8,)),
        ],
    )(
        tile_count,
        *[
            pltpu.with_memory_space_constraint(x, pltpu.HBM)
            for x in (
                tile_owners.reshape(1, tile_total),
                tile_blocks.reshape(1, tile_total),
                tile_contexts.reshape(1, tile_total),
                tile_users.reshape(1, tile_total),
                row_users.reshape(shape),
                row_items.reshape(shape),
                row_contexts.reshape(shape),
                tile_values.reshape(shape),
            )
        ],
    )

    user_steps = halves(lax.axis_size("users"))[::-1]
    if steps:
        came = swap(after(piece, data), "users", steps[0])
    rank_rows = rank_width // items_size
    item_part = take_rows(gram(after(item_factors, (data, piece))), index * rank_rows, rank_rows)
    item_other = swap(item_part, "users", user_steps[0])
    levels = dense_parts(after(profile, item_part), feature_factors, items_size)
    meta_other = swap(meta, "items", top)
    data_other = swap(data, "items", top)
    if steps:
        tables = [jnp.concatenate([piece, after(came, levels[-1])], 0)]
        tables += [swap(tables[0], "users", d) for d in steps[1:2]]
        early = [swap(tables[0], "users", d) for d in steps[2:3]]
    else:
        full = lax.all_gather(piece, "users", tiled=True)
        tables, early = [full.reshape(-1, SLAB, cols).transpose(0, 2, 1)], []
    levels = scatter_levels(levels, order[:-1])
    dense_other = swap(levels[1], "items", top)
    late = after(context_factors, levels[1])
    contexts = lax.dynamic_slice_in_dim(late, high * cols, cols, 1)
    contexts = contexts.reshape(-1, CB, cols).transpose(0, 2, 1)
    context_part = take_rows(gram(late), index * rank_rows, rank_rows)
    if early:
        tables = tables + early + [swap(tables[1], "users", steps[2])]
    item_part = item_part + item_other
    for distance in user_steps[1:]:
        item_part = item_part + swap(item_part, "users", distance)
    if steps:
        for distance in halves(top)[::-1]:
            tables = tables + [swap(x, "items", distance) for x in tables]
    dense = levels[0] + after(dense_other, item_part)
    diagonal = (
        index * rank_rows + lax.broadcasted_iota(jnp.int32, item_part.shape, 0)
        == lax.broadcasted_iota(jnp.int32, item_part.shape, 1)
    ).astype(F32)
    normal = [item_part * context_part + dense[user_rows:] + RIDGE * diagonal]
    data_other = after(data_other, normal[0])
    normal = normal + [swap(normal[0], "items", top)]

    sizes = [s * user_rows for s in level_sizes(items_size)]
    levels = pl.pallas_call(
        lambda *refs: tiles_kernel(len(tables), user_rows, *refs),
        name="tiles",
        out_shape=[pltpu.VMEM((n, cols), F32) for n in sizes],
        in_specs=[ANY] * (5 + len(tables)),
        cost_estimate=cost(15),
        compiler_params=pltpu.CompilerParams(vmem_limit_bytes=VMEM_GRANT),
        out_specs=[VM] * len(sizes),
        scratch_shapes=[
            pltpu.VMEM((sum(t.shape[0] for t in tables), cols, SLAB), BF16),
            pltpu.VMEM((2,) + data.shape, BF16),
            pltpu.VMEM(contexts.shape, BF16),
            pltpu.VMEM((4, 2 * tile_total, width), F32),
            pltpu.VMEM((slab_users, cols), F32),
            pltpu.SMEM(meta.shape, jnp.int32),
            pltpu.SMEM(meta.shape, jnp.int32),
            pltpu.SemaphoreType.DMA((5 + len(tables),)),
        ],
    )(*here(meta, meta_other, data, data_other, contexts, *tables))
    mine, near = scatter_levels(levels, order[:-1])
    other = swap(near, "items", top)
    normal[1] = after(normal[1], levels[0])
    for distance in order[-2::-1]:
        normal = normal + [swap(x, "items", distance) for x in normal]
    normal[0] = after(normal[0], near)
    normal_inverse = inverse(normal, False)
    users_part, *levels = solve_users(mine, other, dense, normal_inverse, items_size)

    levels = scatter_levels(levels, order[:-1])
    users_other = swap(after(users_part, levels[1]), "items", top)
    (part,) = scatter_levels(levels, order[-1:])
    sums = [part]
    for distance in user_steps:
        part = part + swap(part, "users", distance)
        sums.append(part)
    users_other = after(users_other, sums[1])
    user_factors = joined(users_part, users_other, high)
    for distance in order[-2::-1]:
        bit = (lax.axis_index("items") // distance) % 2
        user_factors = joined(user_factors, swap(user_factors, "items", distance), bit)
    feature_right = lax.dot_general(
        profile,
        user_factors,
        (((0,), (0,)), ((), ())),
        preferred_element_type=F32,
    )
    gathered = [part]
    for distance in order[::-1]:
        gathered = gathered + [swap(x, "items", distance) for x in gathered]
    users_me = lax.axis_index("users")
    for distance in user_steps[:-1]:
        half = feature_right.shape[0] // 2
        bit = (users_me // distance) % 2
        keep = take_rows(feature_right, bit * half, half)
        send = take_rows(feature_right, (1 - bit) * half, half)
        feature_right = keep + swap(send, "users", distance)
    gathered[0] = after(gathered[0], feature_right)
    user_inverse = inverse(gathered, True)
    for distance in user_steps[-1:]:
        feature_right = feature_right + swap(feature_right, "users", distance)
    feature_part = jnp.dot(feature_right, user_inverse, precision=HI).astype(BF16)
    feature_new = gather_users(feature_part, user_steps[:-1])
    return (user_factors, feature_new)


def solution(mesh):
    in_specs = (
        P("users", "items", None),
        P("users", "items", None, None),
        P("users", "items", None),
        P("users", "items", None),
        P("users", "items", None, None),
        P("users", "items", None, None),
        P("users", "items", None, None),
        P("users", "items", None, None),
        P("users", "items"),
        P("users", None),
        P(),
        P("users", "items"),
        P("items", None),
    )
    out_specs = (P("users", None), P("items", None))
    return jax.shard_map(local, mesh=mesh, in_specs=in_specs, out_specs=out_specs, check_vma=False)
```

```python
import jax
import jax.numpy as jnp
from jax import lax
from jax.experimental import pallas as pl
from jax.experimental.pallas import tpu as pltpu
from jax.sharding import PartitionSpec as P

CB = 128
IB = 16
UB = 16
SLAB = 128
RIDGE = 1.0
UNROLL = 64
FLOPS_US = 1000000000
VMEM_GRANT = 16 << 20
PIVOTS = 8
HI = lax.Precision.HIGHEST
VM = pl.BlockSpec(memory_space=pltpu.VMEM)
SM = pl.BlockSpec(memory_space=pltpu.SMEM)
ANY = pl.BlockSpec(memory_space=pl.ANY)
HBM = pl.BlockSpec(memory_space=pltpu.HBM)
F32 = jnp.float32
BF16 = jnp.bfloat16


def gram(matrix):
    return lax.dot_general(
        matrix, matrix, (((0,), (0,)), ((), ())), preferred_element_type=F32
    )


def mm(a, b, dims=(((1,), (0,)), ((), ()))):
    return lax.dot_general(a, b, dims, precision=HI, preferred_element_type=F32)


def solve_pivots(d, r):
    n = len(r)
    if n == 1:
        return [r[0] * (1.0 / d[0][0])]
    h = n // 2
    if n == 2:
        p = 1.0 / d[0][0]
        low = d[0][1] * p
        q = 1.0 / (d[1][1] - d[0][1] * low)
        last = (r[1] - low * r[0]) * q
        return [r[0] * p - low * last, last]
    first = [[d[i][j] if j >= i else None for j in range(h)] for i in range(h)]
    cross = [[d[i][h + j] for j in range(h)] for i in range(h)]
    t = solve_pivots(first, r[:h])
    w = [solve_pivots(first, [cross[i][j] for i in range(h)]) for j in range(h)]
    schur = [
        [
            d[h + i][h + j] - sum(cross[m][i] * w[j][m] for m in range(h)) if j >= i else None
            for j in range(h)
        ]
        for i in range(h)
    ]
    rest = [r[h + i] - sum(cross[m][i] * t[m] for m in range(h)) for i in range(h)]
    q = solve_pivots(schur, rest)
    return [t[m] - sum(w[j][m] * q[j] for j in range(h)) for m in range(h)] + q


def base_inverse(a):
    n = a.shape[0]
    lanes = lax.broadcasted_iota(jnp.int32, (PIVOTS, n), 1)
    lane1 = lax.broadcasted_iota(jnp.int32, (1, n), 1)
    blocks = [a[PIVOTS * i : PIVOTS * (i + 1), :] for i in range(n // PIVOTS)]

    def columns(block, k):
        return [jnp.broadcast_to(block[:, k + j : k + j + 1], (PIVOTS, n)) for j in range(PIVOTS)]

    for v in range(n // PIVOTS):
        k = v * PIVOTS
        pivot = columns(blocks[v], k)
        d = [[pivot[j][i : i + 1, :] for j in range(PIVOTS)] for i in range(PIVOTS)]
        inside = (lane1 >= k) & (lane1 < k + PIVOTS)
        r = [
            jnp.where(inside, (lane1 == k + i).astype(F32), blocks[v][i : i + 1, :])
            for i in range(PIVOTS)
        ]
        rows = [jnp.broadcast_to(x, (PIVOTS, n)) for x in solve_pivots(d, r)]
        inside = (lanes >= k) & (lanes < k + PIVOTS)
        new = []
        for i, block in enumerate(blocks):
            if i == v:
                sub = lax.broadcasted_iota(jnp.int32, (PIVOTS, n), 0)
                x = rows[0]
                for j in range(1, PIVOTS):
                    x = jnp.where(sub == j, rows[j], x)
            else:
                c = columns(block, k)
                x = jnp.where(inside, 0.0, block)
                u = c[0] * rows[0]
                for j in range(1, PIVOTS):
                    u = u + c[j] * rows[j]
                x = x - u
            new.append(x)
        blocks = new
    return jnp.concatenate(blocks, 0)


def inverse_value(a):
    n = a.shape[0]
    if n <= 128:
        return base_inverse(a)
    h = n // 2
    a12 = a[:h, h:]
    i11 = inverse_value(a[:h, :h])
    w = mm(i11, a12)
    i22 = inverse_value(a[h:, h:] - mm(a12, w, (((0,), (0,)), ((), ()))))
    nt = (((1,), (1,)), ((), ()))
    b12 = -mm(w, i22)
    b11 = i11 - mm(b12, w, nt)
    return jnp.concatenate(
        [jnp.concatenate([b11, b12], 1), jnp.concatenate([b12.T, i22], 1)], 0
    )


def inverse_kernel(ridge, *refs):
    parts, out, full = refs[:-2], refs[-2], refs[-1]
    index = kernel_ids(0)[3]
    for p, part in enumerate(parts):
        rows = part.shape[0]
        full[pl.ds(pl.multiple_of((p ^ index) * rows, rows), rows), :] = part[...]
    a = full[...]
    if ridge:
        same = lax.broadcasted_iota(jnp.int32, a.shape, 0) == lax.broadcasted_iota(
            jnp.int32, a.shape, 1
        )
        a = a + jnp.where(same, RIDGE, 0.0)
    out[...] = inverse_value(a)


def inverse(parts, ridge):
    n = parts[0].shape[1]
    return pl.pallas_call(
        lambda *refs: inverse_kernel(ridge, *refs),
        out_shape=pltpu.VMEM((n, n), F32),
        in_specs=[VM] * len(parts),
        out_specs=VM,
        cost_estimate=cost(11),
    compiler_params=pltpu.CompilerParams(vmem_limit_bytes=VMEM_GRANT),
        scratch_shapes=[pltpu.VMEM((n, n), F32)],
    )(*here(*parts))


def level_sizes(blocks):
    sizes = [1]
    while sum(sizes) < blocks:
        sizes.append(sum(sizes))
    return sizes


def dense_kernel(blocks, profile, features, *refs):
    ids = kernel_ids(0)
    outs, full = refs[:-1], refs[-1]
    f = features[...]
    full[...] = lax.dot_general(f, f, (((0,), (0,)), ((), ())), preferred_element_type=F32)
    rows, small = profile.shape[0] // blocks, full.shape[0] // blocks
    p = 0
    for out in outs:
        for i in range(out.shape[0] // (rows + small)):
            at = p ^ ids[3]
            start = i * (rows + small)
            out[start : start + rows, :] = jnp.dot(
                profile[pl.ds(pl.multiple_of(at * rows, rows), rows), :],
                f,
                preferred_element_type=F32,
            )
            out[start + rows : start + rows + small, :] = full[
                pl.ds(pl.multiple_of(at * small, small), small), :
            ]
            p += 1


def dense_parts(profile, features, blocks):
    n = features.shape[1]
    rows = profile.shape[0] // blocks + n // blocks
    return pl.pallas_call(
        lambda *refs: dense_kernel(blocks, *refs),
        out_shape=[pltpu.VMEM((s * rows, n), F32) for s in level_sizes(blocks)],
        in_specs=[VM, VM],
        cost_estimate=cost(3.7),
        compiler_params=pltpu.CompilerParams(vmem_limit_bytes=VMEM_GRANT),
        out_specs=[VM] * len(level_sizes(blocks)),
        scratch_shapes=[pltpu.VMEM((n, n), F32)],
    )(*here(profile, features))


def solve_kernel(blocks, mine, other, dense, inverse_ref, users_out, *refs):
    outs, full = refs[:-1], refs[-1]
    ids = kernel_ids(0)
    rows = mine.shape[0]
    first = ids[4] == 0
    left = jnp.where(first, mine[...], other[...])
    right = jnp.where(first, other[...], mine[...])
    total = jnp.concatenate([left, right], 1) + dense[:rows, :]
    users = mm(total, inverse_ref[...]).astype(BF16)
    users_out[...] = users
    full[...] = lax.dot_general(
        users, users, (((0,), (0,)), ((), ())), preferred_element_type=F32
    )
    small = full.shape[0] // blocks
    p = 0
    for out in outs:
        for i in range(out.shape[0] // small):
            at = pl.ds(pl.multiple_of((p ^ ids[3]) * small, small), small)
            out[i * small : (i + 1) * small, :] = full[at, :]
            p += 1


def solve_users(mine, other, dense, normal_inverse, blocks):
    n = normal_inverse.shape[0]
    sizes = level_sizes(blocks)
    return pl.pallas_call(
        lambda *refs: solve_kernel(blocks, *refs),
        out_shape=[pltpu.VMEM((mine.shape[0], n), BF16)]
        + [pltpu.VMEM((s * (n // blocks), n), F32) for s in sizes],
        in_specs=[VM, VM, VM, VM],
        cost_estimate=cost(3),
        compiler_params=pltpu.CompilerParams(vmem_limit_bytes=VMEM_GRANT),
        out_specs=[VM] * (1 + len(sizes)),
        scratch_shapes=[pltpu.VMEM((n, n), F32)],
    )(*here(mine, other, dense, normal_inverse))


def kernel_ids(unit):
    top, _, index = item_order()
    me = lax.axis_index("items")
    return lax.axis_index("users"), index * unit, me % top, index, me // top


def here(*arrays):
    return [pltpu.with_memory_space_constraint(x, pltpu.VMEM) for x in arrays]


def cost(microseconds):
    return pl.CostEstimate(
        flops=int(microseconds * FLOPS_US), bytes_accessed=0, transcendentals=0
    )


def prep_kernel(place, blocks_held, count, *refs):
    inputs, (meta, data), scratch, sems = refs[:8], refs[8:10], refs[10:18], refs[18]
    copies = [
        pltpu.make_async_copy(source, target, sems.at[i])
        for i, (source, target) in enumerate(zip(inputs, scratch))
    ]
    for copy in copies:
        copy.start()
    owners, blocks, contexts, users, ru, ri, rc, val = scratch
    ids = kernel_ids(0)
    tiles_here, width = ru.shape
    for copy in copies:
        copy.wait()
    per_slab = SLAB // IB
    block = owners[...] * blocks_held + blocks[...]
    rows = [
        place(block // per_slab, ids),
        contexts[...],
        users[...] * UB,
        block % per_slab * IB,
        jnp.full((1, tiles_here), count[0, 0], jnp.int32),
    ]
    for i, row in enumerate(rows):
        meta[i : i + 1, :] = row
    meta[len(rows) :, :] = jnp.zeros((8 - len(rows), tiles_here), jnp.int32)
    alive = lax.broadcasted_iota(jnp.int32, (tiles_here, width), 0) < count[0, 0]
    data[0] = ru[...].astype(F32).astype(BF16)
    data[1] = ri[...].astype(F32).astype(BF16)
    data[2] = rc[...].astype(F32).astype(BF16)
    data[3] = jnp.where(alive, val[...].astype(F32), 0.0).astype(BF16)


def tiles_kernel(n_tables, unit, meta_hbm, meta_par_hbm, own_hbm, par_hbm, ctx_hbm, *rest):
    tables = rest[:n_tables]
    outs = rest[n_tables:-8]
    table_ref, raw_ref, ctx_ref, data_ref, acc_ref, meta_own, meta_par, sems = rest[-8:]
    total, width = own_hbm.shape[1:]
    copies = [
        pltpu.make_async_copy(own_hbm, raw_ref.at[0], sems.at[0]),
        pltpu.make_async_copy(par_hbm, raw_ref.at[1], sems.at[1]),
        pltpu.make_async_copy(meta_hbm, meta_own, sems.at[2]),
        pltpu.make_async_copy(meta_par_hbm, meta_par, sems.at[3]),
        pltpu.make_async_copy(ctx_hbm, ctx_ref, sems.at[4]),
    ]
    start = 0
    for i, source in enumerate(tables):
        count = source.shape[0]
        copies.append(
            pltpu.make_async_copy(source, table_ref.at[pl.ds(start, count)], sems.at[5 + i])
        )
        start += count
    for copy in copies:
        copy.start()
    acc_ref[...] = jnp.zeros_like(acc_ref)
    copies[0].wait()
    data_ref[:, :total, :] = raw_ref[0].astype(F32)
    copies[1].wait()
    data_ref[:, total:, :] = raw_ref[1].astype(F32)
    big = lax.broadcasted_iota(jnp.int32, (SLAB, width), 0).astype(F32).astype(BF16)
    wide = lax.broadcasted_iota(jnp.int32, (CB, width), 0).astype(F32).astype(BF16)
    small = lax.broadcasted_iota(jnp.int32, (UB, width), 0).astype(F32).astype(BF16)
    one, zero = jnp.ones((), BF16), jnp.zeros((), BF16)
    flip = kernel_ids(unit)[1]
    copies[2].wait()
    copies[3].wait()
    own_groups = (meta_own[4, 0] + UNROLL - 1) // UNROLL
    groups = own_groups + (meta_par[4, 0] + UNROLL - 1) // UNROLL
    for copy in copies[4:]:
        copy.wait()

    def group(g, _):
        is_own = g < own_groups
        tile = jnp.where(is_own, g, g - own_groups) * UNROLL
        first = pl.multiple_of(tile + jnp.where(is_own, 0, total), UNROLL)
        us, its, cs, vs = (data_ref[j, pl.ds(first, UNROLL), :] for j in range(4))

        def scalar(which, t):
            return jnp.where(is_own, meta_own[which, t], meta_par[which, t])

        for j in range(UNROLL):
            t = tile + j

            def row(x, height):
                return jnp.broadcast_to(x.astype(BF16), (height, width))

            items = its[j : j + 1, :] + scalar(3, t).astype(F32)
            pick_item = jnp.where(row(items, SLAB) == big, one, zero)
            pick_context = jnp.where(row(cs[j : j + 1, :], CB) == wide, one, zero)
            weight = jnp.where(row(us[j : j + 1, :], UB) == small, row(vs[j : j + 1, :], UB), zero)
            a = jnp.dot(table_ref[scalar(0, t)], pick_item, preferred_element_type=F32)
            b = jnp.dot(ctx_ref[scalar(1, t)], pick_context, preferred_element_type=F32)
            p = a * b
            hi = p.astype(BF16)
            lo = (p - hi.astype(F32)).astype(BF16)
            r = lax.dot_general(
                jnp.concatenate([weight, weight], 1),
                jnp.concatenate([hi, lo], 1),
                (((1,), (1,)), ((), ())),
                preferred_element_type=F32,
            )
            at = pl.ds(pl.multiple_of(scalar(2, t) ^ flip, UB), UB)
            acc_ref[at, :] += r
        return 0

    lax.fori_loop(0, groups, group, 0)
    start = 0
    for out in outs:
        out[...] = acc_ref[pl.ds(start, out.shape[0]), :]
        start += out.shape[0]


def swap(x, axis, distance):
    size = lax.axis_size(axis)
    return lax.ppermute(x, axis, [(i, i ^ distance) for i in range(size)])


def halves(size):
    steps = []
    while size > 1:
        size //= 2
        steps.append(size)
    return steps


def take_rows(x, start, count):
    return lax.dynamic_slice_in_dim(x, start, count, 0)


def item_order():
    items_size = lax.axis_size("items")
    top = items_size // 2
    order = halves(top) + [top]
    me = lax.axis_index("items")
    index = 0
    for distance in order:
        index = index * 2 + (me // distance) % 2
    return top, order, index


def after(x, earlier):
    return lax.optimization_barrier((x, earlier))[0]


def scatter_levels(levels, order):
    for distance in order:
        came = swap(levels[-1], "items", distance)
        start, kept = 0, []
        for x in levels[:-1]:
            kept.append(x + came[start : start + x.shape[0]])
            start += x.shape[0]
        levels = kept
    return levels


def joined(x, other, bit):
    return jnp.concatenate([jnp.where(bit == 0, x, other), jnp.where(bit == 0, other, x)], 0)


def gather_users(x, steps):
    me = lax.axis_index("users")
    for distance in steps[::-1]:
        x = joined(x, swap(x, "users", distance), (me // distance) % 2)
    return x


def table_layout(item_factors):
    size = lax.axis_size("users")
    top, _, _ = item_order()
    high = lax.axis_index("items") // top
    low = lax.axis_index("items") % top
    rows, width = item_factors.shape
    cols = width // 2
    if size > 16 or rows % (SLAB * top):
        mine = lax.dynamic_slice_in_dim(item_factors, high * cols, cols, 1)
        return mine, None, lambda slab, ids: slab
    count = rows // top
    mine = lax.dynamic_slice(item_factors, (low * count, high * cols), (count, cols))
    piece = mine.reshape(count // SLAB, SLAB, cols).transpose(0, 2, 1)
    steps = halves(size)
    steps = steps[:1] + steps[:0:-1]
    held, part = rows // SLAB, count // SLAB

    def place(slab, ids):
        owner, inner = slab // held, slab % held
        far = owner ^ ids[0]
        position = sum((far // d % 2) * (1 << n) for n, d in enumerate(steps))
        return ((inner // part ^ ids[2]) * size + position) * part + inner % part

    return piece, steps, place


def local(
    tile_users,
    tile_owners,
    tile_blocks,
    tile_contexts,
    row_users,
    row_items,
    row_contexts,
    tile_values,
    tile_count,
    item_factors,
    context_factors,
    profile,
    feature_factors,
):
    top, order, index = item_order()
    items_size = lax.axis_size("items")
    high = lax.axis_index("items") // top
    tile_total = tile_users.shape[2]
    width = row_users.shape[3]
    rank_width = item_factors.shape[1]
    cols = rank_width // 2
    slab_users = profile.shape[0]
    user_rows = slab_users // items_size
    blocks_held = item_factors.shape[0] // IB
    piece, steps, place = table_layout(item_factors)
    shape = (tile_total, width)
    meta, data = pl.pallas_call(
        lambda *refs: prep_kernel(place, blocks_held, *refs),
        out_shape=(
            pltpu.VMEM((8, tile_total), jnp.int32),
            pltpu.VMEM((4,) + shape, BF16),
        ),
        in_specs=[SM] + [HBM] * 8,
        out_specs=(VM, VM),
        cost_estimate=cost(1.7),
        compiler_params=pltpu.CompilerParams(vmem_limit_bytes=VMEM_GRANT),
        scratch_shapes=[
            *[pltpu.VMEM((1, tile_total), jnp.int32)] * 4,
            *[pltpu.VMEM(shape, jnp.int32)] * 3,
            pltpu.VMEM(shape, BF16),
            pltpu.SemaphoreType.DMA((8,)),
        ],
    )(
        tile_count,
        *[
            pltpu.with_memory_space_constraint(x, pltpu.HBM)
            for x in (
                tile_owners.reshape(1, tile_total),
                tile_blocks.reshape(1, tile_total),
                tile_contexts.reshape(1, tile_total),
                tile_users.reshape(1, tile_total),
                row_users.reshape(shape),
                row_items.reshape(shape),
                row_contexts.reshape(shape),
                tile_values.reshape(shape),
            )
        ],
    )

    user_steps = halves(lax.axis_size("users"))[::-1]
    if steps:
        came = swap(after(piece, data), "users", steps[0])
    rank_rows = rank_width // items_size
    levels = dense_parts(after(profile, (data, piece)), feature_factors, items_size)
    item_part = take_rows(gram(after(item_factors, levels[-1])), index * rank_rows, rank_rows)
    item_other = swap(item_part, "users", user_steps[0])
    meta_other = swap(meta, "items", top)
    data_other = swap(data, "items", top)
    if steps:
        tables = [jnp.concatenate([piece, after(came, item_part)], 0)]
        tables += [swap(tables[0], "users", d) for d in steps[1:2]]
        early = [swap(tables[0], "users", d) for d in steps[2:3]]
    else:
        full = lax.all_gather(piece, "users", tiled=True)
        tables, early = [full.reshape(-1, SLAB, cols).transpose(0, 2, 1)], []
    levels = scatter_levels(levels, order[:-1])
    dense_other = swap(levels[1], "items", top)
    late = after(context_factors, levels[1])
    contexts = lax.dynamic_slice_in_dim(late, high * cols, cols, 1)
    contexts = contexts.reshape(-1, CB, cols).transpose(0, 2, 1)
    context_part = take_rows(gram(late), index * rank_rows, rank_rows)
    if early:
        tables = tables + early + [swap(tables[1], "users", steps[2])]
    item_part = item_part + after(item_other, levels[1])
    for distance in user_steps[1:]:
        item_part = item_part + swap(item_part, "users", distance)
    if steps:
        for distance in halves(top)[::-1]:
            tables = tables + [swap(x, "items", distance) for x in tables]
    dense = levels[0] + after(dense_other, item_part)
    diagonal = (
        index * rank_rows + lax.broadcasted_iota(jnp.int32, item_part.shape, 0)
        == lax.broadcasted_iota(jnp.int32, item_part.shape, 1)
    ).astype(F32)
    normal = [item_part * context_part + dense[user_rows:] + RIDGE * diagonal]
    data_other = after(data_other, normal[0])
    normal = normal + [swap(normal[0], "items", top)]

    sizes = [s * user_rows for s in level_sizes(items_size)]
    levels = pl.pallas_call(
        lambda *refs: tiles_kernel(len(tables), user_rows, *refs),
        name="tiles",
        out_shape=[pltpu.VMEM((n, cols), F32) for n in sizes],
        in_specs=[ANY] * (5 + len(tables)),
        cost_estimate=cost(15),
        compiler_params=pltpu.CompilerParams(vmem_limit_bytes=VMEM_GRANT),
        out_specs=[VM] * len(sizes),
        scratch_shapes=[
            pltpu.VMEM((sum(t.shape[0] for t in tables), cols, SLAB), BF16),
            pltpu.VMEM((2,) + data.shape, BF16),
            pltpu.VMEM(contexts.shape, BF16),
            pltpu.VMEM((4, 2 * tile_total, width), F32),
            pltpu.VMEM((slab_users, cols), F32),
            pltpu.SMEM(meta.shape, jnp.int32),
            pltpu.SMEM(meta.shape, jnp.int32),
            pltpu.SemaphoreType.DMA((5 + len(tables),)),
        ],
    )(*here(meta, meta_other, data, data_other, contexts, *tables))
    mine, near = scatter_levels(levels, order[:-1])
    other = swap(near, "items", top)
    normal[1] = after(normal[1], levels[0])
    for distance in order[-2::-1]:
        normal = normal + [swap(x, "items", distance) for x in normal]
    normal[0] = after(normal[0], near)
    normal_inverse = inverse(normal, False)
    users_part, *levels = solve_users(mine, other, dense, normal_inverse, items_size)

    levels = scatter_levels(levels, order[:-1])
    users_other = swap(users_part, "items", top)
    (part,) = scatter_levels(levels, order[-1:])
    sums = [part]
    for distance in user_steps:
        part = part + swap(part, "users", distance)
        sums.append(part)
    users_other = after(users_other, sums[1])
    user_factors = joined(users_part, users_other, high)
    for distance in order[-2::-1]:
        bit = (lax.axis_index("items") // distance) % 2
        user_factors = joined(user_factors, swap(user_factors, "items", distance), bit)
    feature_right = lax.dot_general(
        profile,
        user_factors,
        (((0,), (0,)), ((), ())),
        preferred_element_type=F32,
    )
    gathered = [part]
    for distance in order[::-1]:
        gathered = gathered + [swap(x, "items", distance) for x in gathered]
    users_me = lax.axis_index("users")
    for distance in user_steps[:-1]:
        half = feature_right.shape[0] // 2
        bit = (users_me // distance) % 2
        keep = take_rows(feature_right, bit * half, half)
        send = take_rows(feature_right, (1 - bit) * half, half)
        feature_right = keep + swap(send, "users", distance)
    gathered[0] = after(gathered[0], feature_right)
    user_inverse = inverse(gathered, True)
    for distance in user_steps[-1:]:
        feature_right = feature_right + swap(feature_right, "users", distance)
    feature_part = jnp.dot(feature_right, user_inverse, precision=HI).astype(BF16)
    feature_new = gather_users(feature_part, user_steps[:-1])
    return (user_factors, feature_new)


def solution(mesh):
    in_specs = (
        P("users", "items", None),
        P("users", "items", None, None),
        P("users", "items", None),
        P("users", "items", None),
        P("users", "items", None, None),
        P("users", "items", None, None),
        P("users", "items", None, None),
        P("users", "items", None, None),
        P("users", "items"),
        P("users", None),
        P(),
        P("users", "items"),
        P("items", None),
    )
    out_specs = (P("users", None), P("items", None))
    return jax.shard_map(local, mesh=mesh, in_specs=in_specs, out_specs=out_specs, check_vma=False)
```

```python
import jax
import jax.numpy as jnp
from jax import lax
from jax.experimental import pallas as pl
from jax.experimental.pallas import tpu as pltpu
from jax.sharding import PartitionSpec as P

CB = 128
IB = 16
UB = 16
SLAB = 128
RIDGE = 1.0
UNROLL = 64
FLOPS_US = 1000000000
VMEM_GRANT = 16 << 20
PIVOTS = 8
HI = lax.Precision.HIGHEST
VM = pl.BlockSpec(memory_space=pltpu.VMEM)
SM = pl.BlockSpec(memory_space=pltpu.SMEM)
ANY = pl.BlockSpec(memory_space=pl.ANY)
HBM = pl.BlockSpec(memory_space=pltpu.HBM)
F32 = jnp.float32
BF16 = jnp.bfloat16


def gram(matrix):
    return lax.dot_general(
        matrix, matrix, (((0,), (0,)), ((), ())), preferred_element_type=F32
    )


def mm(a, b, dims=(((1,), (0,)), ((), ()))):
    return lax.dot_general(a, b, dims, precision=HI, preferred_element_type=F32)


def solve_pivots(d, r):
    n = len(r)
    if n == 1:
        return [r[0] * (1.0 / d[0][0])]
    h = n // 2
    if n == 2:
        p = 1.0 / d[0][0]
        low = d[0][1] * p
        q = 1.0 / (d[1][1] - d[0][1] * low)
        last = (r[1] - low * r[0]) * q
        return [r[0] * p - low * last, last]
    first = [[d[i][j] if j >= i else None for j in range(h)] for i in range(h)]
    cross = [[d[i][h + j] for j in range(h)] for i in range(h)]
    t = solve_pivots(first, r[:h])
    w = [solve_pivots(first, [cross[i][j] for i in range(h)]) for j in range(h)]
    schur = [
        [
            d[h + i][h + j] - sum(cross[m][i] * w[j][m] for m in range(h)) if j >= i else None
            for j in range(h)
        ]
        for i in range(h)
    ]
    rest = [r[h + i] - sum(cross[m][i] * t[m] for m in range(h)) for i in range(h)]
    q = solve_pivots(schur, rest)
    return [t[m] - sum(w[j][m] * q[j] for j in range(h)) for m in range(h)] + q


def base_inverse(a):
    n = a.shape[0]
    lanes = lax.broadcasted_iota(jnp.int32, (PIVOTS, n), 1)
    lane1 = lax.broadcasted_iota(jnp.int32, (1, n), 1)
    blocks = [a[PIVOTS * i : PIVOTS * (i + 1), :] for i in range(n // PIVOTS)]

    def columns(block, k):
        return [jnp.broadcast_to(block[:, k + j : k + j + 1], (PIVOTS, n)) for j in range(PIVOTS)]

    for v in range(n // PIVOTS):
        k = v * PIVOTS
        pivot = columns(blocks[v], k)
        d = [[pivot[j][i : i + 1, :] for j in range(PIVOTS)] for i in range(PIVOTS)]
        inside = (lane1 >= k) & (lane1 < k + PIVOTS)
        r = [
            jnp.where(inside, (lane1 == k + i).astype(F32), blocks[v][i : i + 1, :])
            for i in range(PIVOTS)
        ]
        rows = [jnp.broadcast_to(x, (PIVOTS, n)) for x in solve_pivots(d, r)]
        inside = (lanes >= k) & (lanes < k + PIVOTS)
        new = []
        for i, block in enumerate(blocks):
            if i == v:
                sub = lax.broadcasted_iota(jnp.int32, (PIVOTS, n), 0)
                x = rows[0]
                for j in range(1, PIVOTS):
                    x = jnp.where(sub == j, rows[j], x)
            else:
                c = columns(block, k)
                x = jnp.where(inside, 0.0, block)
                u = c[0] * rows[0]
                for j in range(1, PIVOTS):
                    u = u + c[j] * rows[j]
                x = x - u
            new.append(x)
        blocks = new
    return jnp.concatenate(blocks, 0)


def inverse_value(a):
    n = a.shape[0]
    if n <= 128:
        return base_inverse(a)
    h = n // 2
    a12 = a[:h, h:]
    i11 = inverse_value(a[:h, :h])
    w = mm(i11, a12)
    i22 = inverse_value(a[h:, h:] - mm(a12, w, (((0,), (0,)), ((), ()))))
    nt = (((1,), (1,)), ((), ()))
    b12 = -mm(w, i22)
    b11 = i11 - mm(b12, w, nt)
    return jnp.concatenate(
        [jnp.concatenate([b11, b12], 1), jnp.concatenate([b12.T, i22], 1)], 0
    )


def inverse_kernel(ridge, *refs):
    parts, out, full = refs[:-2], refs[-2], refs[-1]
    index = kernel_ids(0)[3]
    for p, part in enumerate(parts):
        rows = part.shape[0]
        full[pl.ds(pl.multiple_of((p ^ index) * rows, rows), rows), :] = part[...]
    a = full[...]
    if ridge:
        same = lax.broadcasted_iota(jnp.int32, a.shape, 0) == lax.broadcasted_iota(
            jnp.int32, a.shape, 1
        )
        a = a + jnp.where(same, RIDGE, 0.0)
    out[...] = inverse_value(a)


def inverse(parts, ridge):
    n = parts[0].shape[1]
    return pl.pallas_call(
        lambda *refs: inverse_kernel(ridge, *refs),
        out_shape=pltpu.VMEM((n, n), F32),
        in_specs=[VM] * len(parts),
        out_specs=VM,
        cost_estimate=cost(11),
    compiler_params=pltpu.CompilerParams(vmem_limit_bytes=VMEM_GRANT),
        scratch_shapes=[pltpu.VMEM((n, n), F32)],
    )(*here(*parts))


def level_sizes(blocks):
    sizes = [1]
    while sum(sizes) < blocks:
        sizes.append(sum(sizes))
    return sizes


def dense_kernel(blocks, profile, features, *refs):
    ids = kernel_ids(0)
    outs, full = refs[:-1], refs[-1]
    f = features[...]
    full[...] = lax.dot_general(f, f, (((0,), (0,)), ((), ())), preferred_element_type=F32)
    rows, small = profile.shape[0] // blocks, full.shape[0] // blocks
    p = 0
    for out in outs:
        for i in range(out.shape[0] // (rows + small)):
            at = p ^ ids[3]
            start = i * (rows + small)
            out[start : start + rows, :] = jnp.dot(
                profile[pl.ds(pl.multiple_of(at * rows, rows), rows), :],
                f,
                preferred_element_type=F32,
            )
            out[start + rows : start + rows + small, :] = full[
                pl.ds(pl.multiple_of(at * small, small), small), :
            ]
            p += 1


def dense_parts(profile, features, blocks):
    n = features.shape[1]
    rows = profile.shape[0] // blocks + n // blocks
    return pl.pallas_call(
        lambda *refs: dense_kernel(blocks, *refs),
        out_shape=[pltpu.VMEM((s * rows, n), F32) for s in level_sizes(blocks)],
        in_specs=[VM, VM],
        cost_estimate=cost(3.7),
        compiler_params=pltpu.CompilerParams(vmem_limit_bytes=VMEM_GRANT),
        out_specs=[VM] * len(level_sizes(blocks)),
        scratch_shapes=[pltpu.VMEM((n, n), F32)],
    )(*here(profile, features))


def solve_kernel(blocks, mine, other, dense, inverse_ref, users_out, *refs):
    outs, full = refs[:-1], refs[-1]
    ids = kernel_ids(0)
    rows = mine.shape[0]
    first = ids[4] == 0
    left = jnp.where(first, mine[...], other[...])
    right = jnp.where(first, other[...], mine[...])
    total = jnp.concatenate([left, right], 1) + dense[:rows, :]
    users = mm(total, inverse_ref[...]).astype(BF16)
    users_out[...] = users
    full[...] = lax.dot_general(
        users, users, (((0,), (0,)), ((), ())), preferred_element_type=F32
    )
    small = full.shape[0] // blocks
    p = 0
    for out in outs:
        for i in range(out.shape[0] // small):
            at = pl.ds(pl.multiple_of((p ^ ids[3]) * small, small), small)
            out[i * small : (i + 1) * small, :] = full[at, :]
            p += 1


def solve_users(mine, other, dense, normal_inverse, blocks):
    n = normal_inverse.shape[0]
    sizes = level_sizes(blocks)
    return pl.pallas_call(
        lambda *refs: solve_kernel(blocks, *refs),
        out_shape=[pltpu.VMEM((mine.shape[0], n), BF16)]
        + [pltpu.VMEM((s * (n // blocks), n), F32) for s in sizes],
        in_specs=[VM, VM, VM, VM],
        cost_estimate=cost(3),
        compiler_params=pltpu.CompilerParams(vmem_limit_bytes=VMEM_GRANT),
        out_specs=[VM] * (1 + len(sizes)),
        scratch_shapes=[pltpu.VMEM((n, n), F32)],
    )(*here(mine, other, dense, normal_inverse))


def kernel_ids(unit):
    top, _, index = item_order()
    me = lax.axis_index("items")
    return lax.axis_index("users"), index * unit, me % top, index, me // top


def here(*arrays):
    return [pltpu.with_memory_space_constraint(x, pltpu.VMEM) for x in arrays]


def cost(microseconds):
    return pl.CostEstimate(
        flops=int(microseconds * FLOPS_US), bytes_accessed=0, transcendentals=0
    )


def prep_kernel(place, blocks_held, count, *refs):
    inputs, (meta, data), scratch, sems = refs[:8], refs[8:10], refs[10:18], refs[18]
    copies = [
        pltpu.make_async_copy(source, target, sems.at[i])
        for i, (source, target) in enumerate(zip(inputs, scratch))
    ]
    for copy in copies:
        copy.start()
    owners, blocks, contexts, users, ru, ri, rc, val = scratch
    ids = kernel_ids(0)
    tiles_here, width = ru.shape
    for copy in copies:
        copy.wait()
    per_slab = SLAB // IB
    block = owners[...] * blocks_held + blocks[...]
    rows = [
        place(block // per_slab, ids),
        contexts[...],
        users[...] * UB,
        block % per_slab * IB,
        jnp.full((1, tiles_here), count[0, 0], jnp.int32),
    ]
    for i, row in enumerate(rows):
        meta[i : i + 1, :] = row
    meta[len(rows) :, :] = jnp.zeros((8 - len(rows), tiles_here), jnp.int32)
    alive = lax.broadcasted_iota(jnp.int32, (tiles_here, width), 0) < count[0, 0]
    data[0] = ru[...].astype(F32).astype(BF16)
    data[1] = ri[...].astype(F32).astype(BF16)
    data[2] = rc[...].astype(F32).astype(BF16)
    data[3] = jnp.where(alive, val[...].astype(F32), 0.0).astype(BF16)


def tiles_kernel(n_tables, unit, meta_ref, meta_par_ref, own_ref, par_ref, ctx_ref, *rest):
    tables = rest[:n_tables]
    outs = rest[n_tables:-6]
    table_ref, data_ref, acc_ref, meta_own, meta_par, sems = rest[-6:]
    total, width = own_ref.shape[1:]
    copies = [
        pltpu.make_async_copy(meta_ref, meta_own, sems.at[0]),
        pltpu.make_async_copy(meta_par_ref, meta_par, sems.at[1]),
    ]
    for copy in copies:
        copy.start()
    start = 0
    for source in tables:
        table_ref[start : start + source.shape[0]] = source[...]
        start += source.shape[0]
    acc_ref[...] = jnp.zeros_like(acc_ref)
    data_ref[:, :total, :] = own_ref[...].astype(F32)
    data_ref[:, total:, :] = par_ref[...].astype(F32)
    big = lax.broadcasted_iota(jnp.int32, (SLAB, width), 0).astype(F32).astype(BF16)
    wide = lax.broadcasted_iota(jnp.int32, (CB, width), 0).astype(F32).astype(BF16)
    small = lax.broadcasted_iota(jnp.int32, (UB, width), 0).astype(F32).astype(BF16)
    one, zero = jnp.ones((), BF16), jnp.zeros((), BF16)
    flip = kernel_ids(unit)[1]
    for copy in copies:
        copy.wait()
    own_groups = (meta_own[4, 0] + UNROLL - 1) // UNROLL
    groups = own_groups + (meta_par[4, 0] + UNROLL - 1) // UNROLL

    def group(g, _):
        is_own = g < own_groups
        tile = jnp.where(is_own, g, g - own_groups) * UNROLL
        first = pl.multiple_of(tile + jnp.where(is_own, 0, total), UNROLL)
        us, its, cs, vs = (data_ref[j, pl.ds(first, UNROLL), :] for j in range(4))

        def scalar(which, t):
            return jnp.where(is_own, meta_own[which, t], meta_par[which, t])

        for j in range(UNROLL):
            t = tile + j

            def row(x, height):
                return jnp.broadcast_to(x.astype(BF16), (height, width))

            items = its[j : j + 1, :] + scalar(3, t).astype(F32)
            pick_item = jnp.where(row(items, SLAB) == big, one, zero)
            pick_context = jnp.where(row(cs[j : j + 1, :], CB) == wide, one, zero)
            weight = jnp.where(row(us[j : j + 1, :], UB) == small, row(vs[j : j + 1, :], UB), zero)
            a = jnp.dot(table_ref[scalar(0, t)], pick_item, preferred_element_type=F32)
            b = jnp.dot(ctx_ref[scalar(1, t)], pick_context, preferred_element_type=F32)
            p = a * b
            hi = p.astype(BF16)
            lo = (p - hi.astype(F32)).astype(BF16)
            r = lax.dot_general(
                jnp.concatenate([weight, weight], 1),
                jnp.concatenate([hi, lo], 1),
                (((1,), (1,)), ((), ())),
                preferred_element_type=F32,
            )
            at = pl.ds(pl.multiple_of(scalar(2, t) ^ flip, UB), UB)
            acc_ref[at, :] += r
        return 0

    lax.fori_loop(0, groups, group, 0)
    start = 0
    for out in outs:
        out[...] = acc_ref[pl.ds(start, out.shape[0]), :]
        start += out.shape[0]


def swap(x, axis, distance):
    size = lax.axis_size(axis)
    return lax.ppermute(x, axis, [(i, i ^ distance) for i in range(size)])


def halves(size):
    steps = []
    while size > 1:
        size //= 2
        steps.append(size)
    return steps


def take_rows(x, start, count):
    return lax.dynamic_slice_in_dim(x, start, count, 0)


def item_order():
    items_size = lax.axis_size("items")
    top = items_size // 2
    order = halves(top) + [top]
    me = lax.axis_index("items")
    index = 0
    for distance in order:
        index = index * 2 + (me // distance) % 2
    return top, order, index


def after(x, earlier):
    return lax.optimization_barrier((x, earlier))[0]


def scatter_levels(levels, order):
    for distance in order:
        came = swap(levels[-1], "items", distance)
        start, kept = 0, []
        for x in levels[:-1]:
            kept.append(x + came[start : start + x.shape[0]])
            start += x.shape[0]
        levels = kept
    return levels


def joined(x, other, bit):
    return jnp.concatenate([jnp.where(bit == 0, x, other), jnp.where(bit == 0, other, x)], 0)


def gather_users(x, steps):
    me = lax.axis_index("users")
    for distance in steps[::-1]:
        x = joined(x, swap(x, "users", distance), (me // distance) % 2)
    return x


def table_layout(item_factors):
    size = lax.axis_size("users")
    top, _, _ = item_order()
    high = lax.axis_index("items") // top
    low = lax.axis_index("items") % top
    rows, width = item_factors.shape
    cols = width // 2
    if size > 16 or rows % (SLAB * top):
        mine = lax.dynamic_slice_in_dim(item_factors, high * cols, cols, 1)
        return mine, None, lambda slab, ids: slab
    count = rows // top
    mine = lax.dynamic_slice(item_factors, (low * count, high * cols), (count, cols))
    piece = mine.reshape(count // SLAB, SLAB, cols).transpose(0, 2, 1)
    steps = halves(size)
    steps = steps[:1] + steps[:0:-1]
    held, part = rows // SLAB, count // SLAB

    def place(slab, ids):
        owner, inner = slab // held, slab % held
        return ((inner // part ^ ids[2]) * size + (owner ^ ids[0])) * part + inner % part

    return piece, steps, place


def local(
    tile_users,
    tile_owners,
    tile_blocks,
    tile_contexts,
    row_users,
    row_items,
    row_contexts,
    tile_values,
    tile_count,
    item_factors,
    context_factors,
    profile,
    feature_factors,
):
    top, order, index = item_order()
    items_size = lax.axis_size("items")
    high = lax.axis_index("items") // top
    tile_total = tile_users.shape[2]
    width = row_users.shape[3]
    rank_width = item_factors.shape[1]
    cols = rank_width // 2
    slab_users = profile.shape[0]
    user_rows = slab_users // items_size
    blocks_held = item_factors.shape[0] // IB
    piece, steps, place = table_layout(item_factors)
    shape = (tile_total, width)
    meta, data = pl.pallas_call(
        lambda *refs: prep_kernel(place, blocks_held, *refs),
        out_shape=(
            pltpu.VMEM((8, tile_total), jnp.int32),
            pltpu.VMEM((4,) + shape, BF16),
        ),
        in_specs=[SM] + [HBM] * 8,
        out_specs=(VM, VM),
        cost_estimate=cost(1.7),
        compiler_params=pltpu.CompilerParams(vmem_limit_bytes=VMEM_GRANT),
        scratch_shapes=[
            *[pltpu.VMEM((1, tile_total), jnp.int32)] * 4,
            *[pltpu.VMEM(shape, jnp.int32)] * 3,
            pltpu.VMEM(shape, BF16),
            pltpu.SemaphoreType.DMA((8,)),
        ],
    )(
        tile_count,
        *[
            pltpu.with_memory_space_constraint(x, pltpu.HBM)
            for x in (
                tile_owners.reshape(1, tile_total),
                tile_blocks.reshape(1, tile_total),
                tile_contexts.reshape(1, tile_total),
                tile_users.reshape(1, tile_total),
                row_users.reshape(shape),
                row_items.reshape(shape),
                row_contexts.reshape(shape),
                tile_values.reshape(shape),
            )
        ],
    )

    user_steps = halves(lax.axis_size("users"))[::-1]
    first = after(piece, data)
    pieces = {0: piece}
    if steps:
        for d in steps:
            pieces[d] = swap(first, "users", d)
    rank_rows = rank_width // items_size
    levels = dense_parts(after(profile, (data, piece)), feature_factors, items_size)
    item_part = take_rows(gram(after(item_factors, levels[-1])), index * rank_rows, rank_rows)
    item_other = swap(item_part, "users", user_steps[0])
    meta_other = swap(meta, "items", top)
    data_other = swap(data, "items", top)
    if steps:
        for e in sorted(range(1, lax.axis_size("users")), key=lambda e: bin(e).count("1")):
            hops = [d for d in steps if e & d]
            if len(hops) % 2:
                hops = hops[:-2] + hops[:-3:-1]
            if len(hops) > 1:
                pieces[e] = swap(pieces[e ^ hops[-1]], "users", hops[-1])
        tables = [pieces[e] for e in range(lax.axis_size("users"))]
    else:
        full = lax.all_gather(piece, "users", tiled=True)
        tables = [full.reshape(-1, SLAB, cols).transpose(0, 2, 1)]
    levels = scatter_levels(levels, order[:-1])
    dense_other = swap(levels[1], "items", top)
    late = after(context_factors, levels[1])
    contexts = lax.dynamic_slice_in_dim(late, high * cols, cols, 1)
    contexts = contexts.reshape(-1, CB, cols).transpose(0, 2, 1)
    context_part = take_rows(gram(late), index * rank_rows, rank_rows)
    item_part = item_part + after(item_other, levels[1])
    for distance in user_steps[1:]:
        item_part = item_part + swap(item_part, "users", distance)
    if steps:
        for distance in halves(top)[::-1]:
            tables = tables + [
                swap(after(x, contexts) if n == len(tables) // 2 else x, "items", distance)
                for n, x in enumerate(tables)
            ]
    dense = levels[0] + after(dense_other, item_part)
    diagonal = (
        index * rank_rows + lax.broadcasted_iota(jnp.int32, item_part.shape, 0)
        == lax.broadcasted_iota(jnp.int32, item_part.shape, 1)
    ).astype(F32)
    normal = [item_part * context_part + dense[user_rows:] + RIDGE * diagonal]
    data_other = after(data_other, normal[0])
    normal = normal + [swap(normal[0], "items", top)]

    sizes = [s * user_rows for s in level_sizes(items_size)]
    levels = pl.pallas_call(
        lambda *refs: tiles_kernel(len(tables), user_rows, *refs),
        name="tiles",
        out_shape=[pltpu.VMEM((n, cols), F32) for n in sizes],
        in_specs=[VM] * (5 + len(tables)),
        cost_estimate=cost(15),
        compiler_params=pltpu.CompilerParams(vmem_limit_bytes=VMEM_GRANT),
        out_specs=[VM] * len(sizes),
        scratch_shapes=[
            pltpu.VMEM((sum(t.shape[0] for t in tables), cols, SLAB), BF16),
            pltpu.VMEM((4, 2 * tile_total, width), F32),
            pltpu.VMEM((slab_users, cols), F32),
            pltpu.SMEM(meta.shape, jnp.int32),
            pltpu.SMEM(meta.shape, jnp.int32),
            pltpu.SemaphoreType.DMA((2,)),
        ],
    )(*here(meta, meta_other, data, data_other, contexts, *tables))
    mine, near = scatter_levels(levels, order[:-1])
    other = swap(near, "items", top)
    normal[1] = after(normal[1], levels[0])
    for distance in order[-2::-1]:
        normal = normal + [swap(x, "items", distance) for x in normal]
    normal[0] = after(normal[0], near)
    normal_inverse = inverse(normal, False)
    users_part, *levels = solve_users(mine, other, dense, normal_inverse, items_size)

    levels = scatter_levels(levels, order[:-1])
    users_other = swap(users_part, "items", top)
    (part,) = scatter_levels(levels, order[-1:])
    sums = [part]
    for distance in user_steps:
        part = part + swap(part, "users", distance)
        sums.append(part)
    users_other = after(users_other, sums[1])
    user_factors = joined(users_part, users_other, high)
    for distance in order[-2::-1]:
        bit = (lax.axis_index("items") // distance) % 2
        user_factors = joined(user_factors, swap(user_factors, "items", distance), bit)
    feature_right = lax.dot_general(
        profile,
        user_factors,
        (((0,), (0,)), ((), ())),
        preferred_element_type=F32,
    )
    gathered = [part]
    for distance in order[::-1]:
        gathered = gathered + [swap(x, "items", distance) for x in gathered]
    users_me = lax.axis_index("users")
    for distance in user_steps[:-1]:
        half = feature_right.shape[0] // 2
        bit = (users_me // distance) % 2
        keep = take_rows(feature_right, bit * half, half)
        send = take_rows(feature_right, (1 - bit) * half, half)
        feature_right = keep + swap(send, "users", distance)
    gathered[0] = after(gathered[0], feature_right)
    user_inverse = inverse(gathered, True)
    for distance in user_steps[-1:]:
        feature_right = feature_right + swap(feature_right, "users", distance)
    feature_part = jnp.dot(feature_right, user_inverse, precision=HI).astype(BF16)
    feature_new = gather_users(feature_part, user_steps[:-1])
    return (user_factors, feature_new)


def solution(mesh):
    in_specs = (
        P("users", "items", None),
        P("users", "items", None, None),
        P("users", "items", None),
        P("users", "items", None),
        P("users", "items", None, None),
        P("users", "items", None, None),
        P("users", "items", None, None),
        P("users", "items", None, None),
        P("users", "items"),
        P("users", None),
        P(),
        P("users", "items"),
        P("items", None),
    )
    out_specs = (P("users", None), P("items", None))
    return jax.shard_map(local, mesh=mesh, in_specs=in_specs, out_specs=out_specs, check_vma=False)
```
